512 devices in a mesh: outer: 32 (over y, x, core), inner: 16 (over z).
Axes of the slice: x: 4, y: 4, z: 16, core: 2. Of those that a mesh axis runs over, the one named last changes fastest.
Arguments:
- right_sides: float32 [65536, 128], P(('outer', 'inner')), may hold values from -6 to 6
- leaf_order: int32 [512, 128], P(('outer', 'inner')), may hold values from 0 to 127, each once within a row
- leaf_inverse: float32 [65536, 128], P(('outer', 'inner')), may hold values from -0.1237436867076458 to 2.5, as said below
- basis_blocks: float32 [9, 65536, 128], P(None, ('outer', 'inner')), may hold values from -0.25013902 to 0.25013902
Outputs:
- solution: float32 [65536, 128], P(('outer', 'inner'))
The draws below stay inside these ranges and needn't reach their ends.
Inputs may be any that keep to these rules, and one draw needn't show every extreme that they name: `leaf_inverse`: each leaf's block is lower triangular, its diagonal between 1.5 and 2.5.
All inputs are finite; a program needn't handle non-finite values.
Results may differ from the reference program's by a relative error of at most 0.00013.
Values sent between devices are 32-bit elements; how exact they have to be, the bound alone decides.
No kernel may reach another device: no remote copies, remote signals or barrier semaphores. Data moves between devices by JAX's collectives and lax.ppermute only.
A program may use at most 64 MiB of HBM per device.

```python
import math
import jax
import jax.numpy as jnp
from jax import lax

LEAF = 128
RANK = 128
NRHS = 128
LEVELS = 9
ORDER = 65536
N_OUTER = 32
N_INNER = 16
DEVICES = 512


def draw_leaf_inverse(key, part):
    below_key = jax.random.fold_in(key, 11)
    diag_key = jax.random.fold_in(key, 12)
    row_pos = jnp.arange(ORDER, dtype=jnp.int32)[:, None] % LEAF
    col_pos = jnp.arange(LEAF, dtype=jnp.int32)[None, :]
    below = jnp.clip(jax.random.normal(below_key, (ORDER, LEAF), jnp.float32), -4.0, 4.0) * (0.35 / math.sqrt(LEAF))
    diagonal = jax.random.uniform(diag_key, (ORDER, LEAF), jnp.float32, 1.5, 2.5)
    return jnp.where(row_pos == col_pos, diagonal, jnp.where(row_pos > col_pos, below, 0.0))


def draw_basis_blocks(key, part):
    basis_key = jax.random.fold_in(key, 21)
    heights = jnp.arange(LEVELS, dtype=jnp.float32)[:, None, None]
    spread = jnp.sqrt(0.5 / (LEAF * jnp.exp2(heights)))
    raw_values = jnp.clip(jax.random.normal(basis_key, (LEVELS, ORDER, RANK), jnp.float32), -4.0, 4.0)
    return raw_values * spread


def shard_levels(key, shape, split, low, top_value):
    factor_of = 1.0
    for dim, shards_of in split:
        draws = jax.random.uniform(jax.random.fold_in(jax.random.fold_in(key, 6), dim), (shards_of,), jnp.float32, low / len(split), top_value / len(split))
        factor_of = factor_of * jnp.repeat(jnp.exp(draws), shape[dim] // shards_of).reshape((-1,) + (1,) * (len(shape) - 1 - dim))
    return factor_of


def centred(own_key, dims, scale, reach, split=(), kind=jnp.bfloat16):
    entries = jax.random.normal(own_key, dims, jnp.float32) * scale
    if len(split) > 0:
        entries = shard_levels(own_key, dims, split, -0.22, 0.18) * entries
    return jnp.clip(entries, min=-reach, max=reach).astype(kind)


def setup_inputs(seed: int = 0) -> dict:
    seeds = jax.random.split(jax.random.key(seed), 5)
    right_sides = centred(seeds[0], (ORDER, NRHS), 1.0, 6.0, ((0, 512),), jnp.float32)
    leaf_order = jax.vmap(lambda own: jax.random.permutation(own, LEAF))(jax.random.split(seeds[1], DEVICES)).reshape((DEVICES, LEAF)).astype(jnp.int32)
    leaf_inverse = draw_leaf_inverse(jax.random.fold_in(seeds[4], 71), 0)
    basis_blocks = draw_basis_blocks(jax.random.fold_in(seeds[4], 71), 0)
    return dict(right_sides=right_sides, leaf_order=leaf_order, leaf_inverse=leaf_inverse, basis_blocks=basis_blocks)


def coupling_inverse(size):
    unit = jnp.eye(size, dtype=jnp.float32)
    return jnp.block([[2.0 * unit, -unit], [-unit, 2.0 * unit]]) / 3.0

def reference(right_sides, leaf_order, leaf_inverse, basis_blocks):
    leaves = N_OUTER * N_INNER
    sides = right_sides.reshape(leaves, LEAF, NRHS)
    tree_sides = jnp.take_along_axis(sides, leaf_order[:, :, None], axis=1)
    basis_cols = basis_blocks.reshape(LEVELS, leaves, LEAF, RANK).transpose(1, 2, 0, 3).reshape(leaves, LEAF, LEVELS * RANK)
    columns = jnp.concatenate([basis_cols, tree_sides], axis=2)
    factor = leaf_inverse.reshape(leaves, LEAF, LEAF)
    inner_product = jnp.einsum('jpq,jqc->jpc', factor, columns, precision=lax.Precision.HIGHEST)
    applied = jnp.einsum('jqp,jqc->jpc', factor, inner_product, precision=lax.Precision.HIGHEST)
    coupling = coupling_inverse(RANK)
    for height in range(LEVELS):
        basis_now = basis_blocks[height].reshape(leaves, LEAF, RANK)
        column_count = applied.shape[2]
        products = jnp.einsum('jpr,jpc->jrc', basis_now, applied, precision=lax.Precision.HIGHEST)
        child_sums = products.reshape(leaves >> height, 1 << height, RANK, column_count).sum(axis=1)
        paired = child_sums.reshape(leaves >> height + 1, 2, RANK, column_count)
        gram_first = paired[:, 0, :, :RANK]
        gram_second = paired[:, 1, :, :RANK]
        zero_block = jnp.zeros_like(gram_first)
        system = coupling[None] + jnp.concatenate([jnp.concatenate([gram_first, zero_block], axis=2), jnp.concatenate([zero_block, gram_second], axis=2)], axis=1)
        targets = paired[:, :, :, RANK:].reshape(leaves >> height + 1, 2 * RANK, column_count - RANK)
        factor_low = jnp.linalg.cholesky(system)
        middle = jax.scipy.linalg.solve_triangular(factor_low, targets, lower=True)
        weights = jax.scipy.linalg.solve_triangular(factor_low, middle, lower=True, trans=1)
        weights = weights.reshape(leaves >> height, RANK, column_count - RANK)
        per_leaf = jnp.repeat(weights, 1 << height, axis=0)
        applied = applied[:, :, RANK:] - jnp.einsum('jpr,jrc->jpc', applied[:, :, :RANK], per_leaf, precision=lax.Precision.HIGHEST)
    rows_index = jnp.arange(leaves, dtype=jnp.int32)[:, None]
    solution = jnp.zeros_like(sides).at[rows_index, leaf_order].set(applied)
    return solution.reshape(leaves * LEAF, NRHS)
```

```python
import functools

import jax
import jax.numpy as jnp
from jax import lax
from jax.experimental import pallas as pl
from jax.experimental.pallas import tpu as pltpu
from jax.sharding import PartitionSpec as P

B = 128
F32 = jnp.float32


def mm(a, b):
    return jnp.dot(a, b, precision=lax.Precision.HIGHEST, preferred_element_type=F32)


def tn(a, b):
    return lax.dot_general(
        a, b, (((0,), (0,)), ((), ())), precision=lax.Precision.HIGHEST, preferred_element_type=F32
    )


def eye():
    return (
        lax.broadcasted_iota(jnp.int32, (B, B), 0) == lax.broadcasted_iota(jnp.int32, (B, B), 1)
    ).astype(F32)


def sl(i, j):
    return slice(i * B, j * B)


def unit_inverse(grams, x_ref, r_ref):
    unit = eye()
    count = len(grams)
    h = jnp.ones((1, 1), F32)
    for g in grams:
        h = jnp.maximum(
            h, jnp.max(jnp.sum(jnp.abs(g), axis=0, keepdims=True), axis=1, keepdims=True)
        )
    s = 2.0 / h
    s = 2.0 * s * (s + 2.0)
    left = jnp.zeros((1, 1), jnp.int32)
    ahead = s
    for _ in range(14):
        left = left + (ahead < 4000.0).astype(jnp.int32)
        ahead = 2.0 * ahead * (ahead + 2.0)
    steps = jnp.max(left)
    inv_t = 1.0 / (1.0 + s)
    c = 1.0 + inv_t
    scale = 2.0 / (h + 2.0)
    for k, g in enumerate(grams):
        r = (h * unit - 2.0 * g) / (h + 2.0)
        x_ref[k] = (c * scale) * (unit + r)
        r_ref[k] = c * mm(r, r) - inv_t * unit

    def double(_, s):
        s = 2.0 * s * (s + 2.0)
        inv_t = 1.0 / (1.0 + s)
        c = 1.0 + inv_t
        for k in range(count):
            r = r_ref[k]
            x = x_ref[k]
            x_ref[k] = c * (x + mm(x, r))
            r_ref[k] = c * mm(r, r) - inv_t * unit
        return s

    lax.fori_loop(0, steps, double, s)
    found = []
    for k, g in enumerate(grams):
        x = x_ref[k]
        found.append(x + mm(x, unit - x - mm(g, x)))
    return found


def pair_inverse(s_first, s_second):
    unit = eye()
    r = 0.5 * (s_first + s_second - unit)
    t = 7.0
    x = (0.5 * (1.0 + 1.0 / t)) * (unit + r)
    r = (1.0 + 1.0 / t) * mm(r, r) - (1.0 / t) * unit
    for last in (False, False, True):
        t = 2.0 * t * t - 1.0
        c = 1.0 + 1.0 / t
        x = c * (x + mm(x, r))
        if not last:
            r = c * mm(r, r) - (1.0 / t) * unit
    return x


def leaf_kernel(nb, order_ref, r_ref, u_ref, rhs_ref, z_ref, x_scr, r_scr):
    pick = (lax.broadcasted_iota(jnp.int32, (B, B), 0) == order_ref[...]).astype(F32)
    r = r_ref[...]
    for b in range(nb - 1):
        z_ref[:, sl(b, b + 1)] = mm(r, u_ref[b])
    z_ref[:, sl(nb - 1, nb)] = mm(r, tn(pick, rhs_ref[...]))
    z0 = z_ref[:, sl(0, 1)]
    (s,) = unit_inverse([tn(z0, z0)], x_scr, r_scr)
    z_ref[:, sl(nb, nb + 1)] = s


def quad_kernel(nb, slots, table_ref, zs0, zs1, zs2, zs3, act_ref, pas_ref, own_ref, z, y, w, x1, m2_scr, n2_scr, x_scr, r_scr, sem):
    last = nb - 1
    copies = [
        pltpu.make_async_copy(src, z.at[pl.ds(i * B, B)], sem.at[i])
        for i, src in enumerate((zs0, zs1, zs2, zs3))
    ]
    for copy in copies:
        copy.start()
    for copy in copies:
        copy.wait()
    w0 = (nb - 1) * B

    def first(i, carry):
        rows = pl.ds(pl.multiple_of(i * B, B), B)
        p = tn(z[rows, sl(0, 1)], z[rows, sl(1, nb)])
        w[rows, :] = mm(z[rows, sl(nb, nb + 1)], p)
        return carry

    lax.fori_loop(0, 4, first, 0)
    for n in range(2):
        a, b = slice(2 * n * B, (2 * n + 1) * B), slice((2 * n + 1) * B, (2 * n + 2) * B)
        t = pair_inverse(z[a, sl(nb, nb + 1)], z[b, sl(nb, nb + 1)])
        x1[n] = mm(t, w[a, :] + w[b, :])

    def second(i, carry):
        rows = pl.ds(pl.multiple_of(i * B, B), B)
        x = x1[i // 2]
        weights = w[rows, :] + mm(z[rows, sl(nb, nb + 1)], x)
        y[rows, sl(1, nb)] = z[rows, sl(1, nb)] - mm(z[rows, sl(0, 1)], weights)
        return carry

    lax.fori_loop(0, 4, second, 0)
    rows = [slice(0, 2 * B), slice(2 * B, 4 * B)]
    m = [tn(z[rows[n], sl(1, 2)], y[rows[n], sl(1, nb)]) for n in range(2)]
    s = unit_inverse([m[n][:, :B] for n in range(2)], x_scr, r_scr)
    nn = [mm(s[n], m[n][:, B:]) for n in range(2)]
    x = mm(pair_inverse(s[0], s[1]), nn[0] + nn[1])
    for n in range(2):
        weights = nn[n] + mm(s[n], x)
        y[rows[n], sl(2, nb)] = y[rows[n], sl(2, nb)] - mm(y[rows[n], sl(1, 2)], weights)
    m2 = tn(z[:, sl(2, 3)], y[:, sl(2, nb)])
    (s2,) = unit_inverse([m2[:, :B]], x_scr, r_scr)
    n2 = mm(s2, m2[:, B:])
    m2_scr[...] = m2
    n2_scr[...] = n2
    m3 = tn(z[:, sl(3, 4)], y[:, sl(3, nb)]) - tn(m2[:, sl(1, 2)], n2)
    wide = nb - 3
    act_ref[:, sl(0, 1)] = s2
    act_ref[:, sl(1, 1 + wide)] = n2
    act_ref[:, sl(1 + wide, 1 + 2 * wide)] = m3
    total = act_ref.shape[1] // B
    if total > 1 + 2 * wide:
        act_ref[:, sl(1 + 2 * wide, total)] = jnp.zeros((B, (total - 1 - 2 * wide) * B), F32)
    y2 = y[0:B, sl(2, 3)]
    own_ref[:, sl(1, nb - 2)] = y[0:B, sl(3, nb)] - mm(y2, n2)
    own_ref[:, sl(0, 1)] = mm(y2, s2)

    def passive(k, carry):
        a = table_ref[0, k]
        b = table_ref[1, k]

        def at(block):
            return pl.ds(pl.multiple_of(block * B, B), B)

        pas_ref[:, at(k)] = tn(z[:, at(a)], y[:, at(b)]) - tn(m2_scr[:, at(a - 2)], n2_scr[:, at(b - 3)])
        return carry

    lax.fori_loop(0, slots, passive, 0)


def ring_kernel(nb, share, slots, side_ref, act_ref, own_ref, pay_ref, out_ref, la, lb, q, m, nn, tot, x_scr, r_scr, s_scr):
    wide = nb - 3
    deep = nb - 4

    def piece(group, k):
        return act_ref[4 * group + k // share, :, sl(k % share, k % share + 1)]

    for node in range(2):
        g, h = 2 * node, 2 * node + 1
        for k in range(wide):
            q[node, :, sl(k, k + 1)] = piece(g, 1 + k) + piece(h, 1 + k)
        t = pair_inverse(piece(g, 0), piece(h, 0))
        x = mm(t, q[node])
        m[node] = x
        lb[sl(node, node + 1), :] = x[:, B:]
        la[sl(node, node + 1), :] = q[node, :, B:]
        m3 = tn(q[node, :, :B], x)
        for k in range(wide):
            nn[node, :, sl(k, k + 1)] = (
                piece(g, 1 + wide + k) + piece(h, 1 + wide + k) - m3[:, sl(k, k + 1)]
            )
    s = unit_inverse([nn[0, :, :B], nn[1, :, :B]], x_scr, r_scr)
    for node in range(2):
        s_scr[node] = s[node]
        la[sl(2 + node, 3 + node), :] = nn[node, :, B:]
        lb[sl(2 + node, 3 + node), :] = mm(s[node], nn[node, :, B:])
    q3 = lb[sl(2, 3), :] + lb[sl(3, 4), :]
    x3 = mm(pair_inverse(s[0], s[1]), q3)
    la[sl(4, 5), :] = q3
    lb[sl(4, 5), :] = x3
    at = 0
    for k in range(deep - 1):
        for b in range(k, deep):
            who, slot = (at + b - k) // slots, share + (at + b - k) % slots
            tot[:, sl(at + b - k, at + b - k + 1)] = (
                act_ref[who, :, sl(slot, slot + 1)]
                + act_ref[4 + who, :, sl(slot, slot + 1)]
                + act_ref[8 + who, :, sl(slot, slot + 1)]
                + act_ref[12 + who, :, sl(slot, slot + 1)]
            )
        part = sl(at, at + deep - k)
        tot[:, part] = tot[:, part] - tn(la[:, sl(k, k + 1)], lb[:, sl(k, deep)])
        at += deep - k

    def panel(a):
        at = sum(nb - k for k in range(4, a))
        return tot[:, sl(at, at + nb - a)]

    own_side(nb, 4, panel, pay_ref, x_scr, r_scr)
    side = side_ref[0]
    y = own_ref[:, sl(1, nb - 2)] - mm(own_ref[:, :B], m[side])
    n3 = lb[pl.ds(pl.multiple_of((2 + side) * B, B), B), :]
    weights = n3 + mm(s_scr[side], x3)
    out_ref[...] = y[:, B:] - mm(y[:, :B], weights)


def own_side(nb, level, m, pay_ref, x_scr, r_scr):
    row = m(level)
    wide = nb - 1 - level
    (s,) = unit_inverse([row[:, :B]], x_scr, r_scr)
    n = mm(s, row[:, B:])
    pay_ref[:, sl(0, 1)] = s
    pay_ref[:, sl(1, 1 + wide)] = n
    at = 1 + wide
    for a in range(level + 1, nb - 1):
        k = a - level
        pay_ref[:, sl(at, at + nb - a)] = m(a) - tn(
            row[:, sl(k, k + 1)], n[:, sl(k - 1, wide)]
        )
        at += nb - a


def merge_kernel(nb, level, own_ref, other_ref, pay_ref, x_ref, x_scr, r_scr):
    wide = nb - 1 - level
    q = own_ref[:, sl(1, 1 + wide)] + other_ref[:, sl(1, 1 + wide)]
    x = mm(pair_inverse(own_ref[:, :B], other_ref[:, :B]), q)
    x_ref[...] = x

    def panel(a):
        k = a - level - 1
        at = 1 + wide + sum(nb - j for j in range(level + 1, a))
        part = sl(at, at + nb - a)
        return own_ref[:, part] + other_ref[:, part] - tn(q[:, sl(k, k + 1)], x[:, sl(k, wide)])

    own_side(nb, level + 1, panel, pay_ref, x_scr, r_scr)


def update_kernel(pay_ref, x_ref, y_ref, out_ref):
    wide = x_ref.shape[1]
    weights = pay_ref[:, B : B + wide] + mm(pay_ref[:, :B], x_ref[...])
    out_ref[...] = y_ref[:, B:] - mm(y_ref[:, :B], weights)


def finish_kernel(order_ref, r_ref, own_ref, other_ref, y_ref, out_ref):
    s = own_ref[:, :B]
    n = own_ref[:, B:]
    x = mm(pair_inverse(s, other_ref[:, :B]), n + other_ref[:, B:])
    y = y_ref[:, B:] - mm(y_ref[:, :B], n + mm(s, x))
    pick = (lax.broadcasted_iota(jnp.int32, (B, B), 0) == order_ref[...]).astype(F32)
    out_ref[...] = mm(pick, tn(r_ref[...], y))


def call(kernel, out_widths, args, scratch=(), in_specs=None, interpret=False):
    shapes = [jax.ShapeDtypeStruct((B, w * B), F32) for w in out_widths]
    vmem = pl.BlockSpec(memory_space=pltpu.VMEM)
    one = len(shapes) == 1
    return pl.pallas_call(
        kernel,
        out_shape=shapes[0] if one else shapes,
        in_specs=[vmem] * len(args) if in_specs is None else in_specs,
        out_specs=vmem if one else [vmem] * len(shapes),
        scratch_shapes=list(scratch),
        interpret=interpret,
    )(*args)


def swapped(block, axis, bit):
    count = lax.axis_size(axis)
    return lax.ppermute(block, axis, [(k, k ^ (1 << bit)) for k in range(count)])


def pay_width(levels, level):
    return 1 + (levels - level) + sum(levels + 1 - a for a in range(level + 1, levels))


def body(right_sides, leaf_order, leaf_inverse, basis_blocks, interpret=False):
    run = functools.partial(call, interpret=interpret)
    part = functools.partial
    levels = basis_blocks.shape[0]
    nb = levels + 1
    two = [pltpu.VMEM((2, B, B), F32)] * 2
    vmem = pl.BlockSpec(memory_space=pltpu.VMEM)
    anywhere = pl.BlockSpec(memory_space=pl.ANY)

    z0 = run(part(leaf_kernel, nb), [nb + 1], [leaf_order, leaf_inverse, basis_blocks, right_sides], two)
    z1 = swapped(z0, "inner", 0)
    z2 = swapped(z0, "inner", 1)
    z3 = swapped(z2, "inner", 0)

    active = 1 + 2 * (nb - 3)
    share = -(-active // 4)
    pairs = [(a, b) for a in range(4, levels) for b in range(a, nb)]
    slots = -(-len(pairs) // 4)
    pairs = pairs + [pairs[-1]] * (4 * slots - len(pairs))
    table = jnp.array(pairs, jnp.int32).reshape(4, slots, 2)
    place = lax.axis_index("inner")
    mine = lax.dynamic_index_in_dim(table, place & 3, 0, keepdims=False).T
    smem = pl.BlockSpec(memory_space=pltpu.SMEM)
    act, pas, own = run(
        part(quad_kernel, nb, slots),
        [4 * share, slots, nb - 2],
        [mine, z0, z1, z2, z3],
        [
            pltpu.VMEM((4 * B, (nb + 1) * B), F32),
            pltpu.VMEM((4 * B, nb * B), F32),
            pltpu.VMEM((4 * B, (nb - 1) * B), F32),
            pltpu.VMEM((2, B, (nb - 1) * B), F32),
            pltpu.VMEM((B, (nb - 2) * B), F32),
            pltpu.VMEM((B, (nb - 3) * B), F32),
            *two,
            pltpu.SemaphoreType.DMA((4,)),
        ],
        [smem] + [anywhere] * 4,
    )
    act = lax.dynamic_slice(act, (0, (place & 3) * (share * B)), (B, share * B))
    gathered = lax.all_gather(jnp.concatenate([act, pas], axis=1), "inner")
    side = (place >> 3).astype(jnp.int32).reshape(1)
    pay, y = run(
        part(ring_kernel, nb, share, slots),
        [pay_width(levels, 4), nb - 4],
        [side, gathered, own],
        [
            pltpu.VMEM((5 * B, (nb - 4) * B), F32),
            pltpu.VMEM((5 * B, (nb - 4) * B), F32),
            pltpu.VMEM((2, B, (nb - 3) * B), F32),
            pltpu.VMEM((2, B, (nb - 3) * B), F32),
            pltpu.VMEM((2, B, (nb - 3) * B), F32),
            pltpu.VMEM((B, len(pairs) * B), F32),
            *two,
            pltpu.VMEM((2, B, B), F32),
        ],
        [smem, vmem, vmem],
    )

    for level in range(4, levels - 1):
        other = swapped(pay, "outer", level - 4)
        after, x = run(
            part(merge_kernel, nb, level), [pay_width(levels, level + 1), levels - level], [pay, other], two
        )
        y = run(update_kernel, [levels - level], [pay[:, : (1 + levels - level) * B], x, y])
        pay = after
    other = swapped(pay, "outer", levels - 5)
    return run(finish_kernel, [1], [leaf_order, leaf_inverse, pay, other, y])


def solution(mesh):
    in_specs = (
        P(("outer", "inner"), None),
        P(("outer", "inner"), None),
        P(("outer", "inner"), None),
        P(None, ("outer", "inner"), None),
    )
    out_specs = P(("outer", "inner"), None)
    return jax.shard_map(body, mesh=mesh, in_specs=in_specs, out_specs=out_specs, check_vma=False)
```

```python
import functools

import jax
import jax.numpy as jnp
from jax import lax
from jax.experimental import pallas as pl
from jax.experimental.pallas import tpu as pltpu
from jax.sharding import PartitionSpec as P

B = 128
F32 = jnp.float32


HIGH = lax.Precision.HIGHEST
HALF = jnp.bfloat16


def halves(a):
    top = a.astype(HALF)
    return top, (a - top.astype(F32)).astype(HALF)


def product(a, b, dims):
    def dot(x, y):
        return lax.dot_general(x, y, (dims, ((), ())), preferred_element_type=F32)

    a_top, a_low = halves(a)
    b_top, b_low = halves(b)
    return dot(a_top, b_top) + (dot(a_top, b_low) + dot(a_low, b_top))


def mm(a, b):
    return product(a, b, ((1,), (0,)))


def tn(a, b):
    return product(a, b, ((0,), (0,)))


def exact(a, b):
    return jnp.dot(a, b, precision=HIGH, preferred_element_type=F32)


def exact_tn(a, b):
    return lax.dot_general(
        a, b, (((0,), (0,)), ((), ())), precision=HIGH, preferred_element_type=F32
    )


def eye():
    return (
        lax.broadcasted_iota(jnp.int32, (B, B), 0) == lax.broadcasted_iota(jnp.int32, (B, B), 1)
    ).astype(F32)


def sl(i, j):
    return slice(i * B, j * B)


def unit_inverse(grams, x_ref, r_ref):
    unit = eye()
    count = len(grams)
    h = jnp.ones((1, 1), F32)
    for g in grams:
        h = jnp.maximum(
            h, jnp.max(jnp.sum(jnp.abs(g), axis=0, keepdims=True), axis=1, keepdims=True)
        )
    s = 2.0 / h
    s = 2.0 * s * (s + 2.0)
    left = jnp.zeros((1, 1), jnp.int32)
    ahead = s
    for _ in range(14):
        left = left + (ahead < 4000.0).astype(jnp.int32)
        ahead = 2.0 * ahead * (ahead + 2.0)
    steps = jnp.max(left)
    inv_t = 1.0 / (1.0 + s)
    c = 1.0 + inv_t
    scale = 2.0 / (h + 2.0)
    for k, g in enumerate(grams):
        r = (h * unit - 2.0 * g) / (h + 2.0)
        x_ref[k] = (c * scale) * (unit + r)
        r_ref[k] = c * mm(r, r) - inv_t * unit

    def double(_, s):
        s = 2.0 * s * (s + 2.0)
        inv_t = 1.0 / (1.0 + s)
        c = 1.0 + inv_t
        for k in range(count):
            r = r_ref[k]
            x = x_ref[k]
            x_ref[k] = c * (x + mm(x, r))
            r_ref[k] = c * mm(r, r) - inv_t * unit
        return s

    lax.fori_loop(0, steps, double, s)
    found = []
    for k, g in enumerate(grams):
        x = x_ref[k]
        found.append(x + mm(x, unit - x - exact(g, x)))
    return found


def pair_inverse(s_first, s_second):
    unit = eye()
    r = 0.5 * (s_first + s_second - unit)
    t = 7.0
    x = (0.5 * (1.0 + 1.0 / t)) * (unit + r)
    r = (1.0 + 1.0 / t) * mm(r, r) - (1.0 / t) * unit
    for last in (False, False, True):
        t = 2.0 * t * t - 1.0
        c = 1.0 + 1.0 / t
        x = c * (x + mm(x, r))
        if not last:
            r = c * mm(r, r) - (1.0 / t) * unit
    return x


def leaf_kernel(nb, order_ref, r_ref, u_ref, rhs_ref, z_ref, x_scr, r_scr):
    pick = (lax.broadcasted_iota(jnp.int32, (B, B), 0) == order_ref[...]).astype(F32)
    r = r_ref[...]
    for b in range(nb - 1):
        z_ref[:, sl(b, b + 1)] = mm(r, u_ref[b])
    z_ref[:, sl(nb - 1, nb)] = mm(r, exact_tn(pick, rhs_ref[...]))
    z0 = z_ref[:, sl(0, 1)]
    (s,) = unit_inverse([tn(z0, z0)], x_scr, r_scr)
    z_ref[:, sl(nb, nb + 1)] = s


def pair_kernel(nb, first_ref, second_ref, y_ref):
    refs = (first_ref, second_ref)
    n = [
        exact(z[:, sl(nb, nb + 1)], tn(z[:, sl(0, 1)], z[:, sl(1, nb)]))
        for z in refs
    ]
    t = pair_inverse(first_ref[:, sl(nb, nb + 1)], second_ref[:, sl(nb, nb + 1)])
    x = mm(t, n[0] + n[1])
    for i, z in enumerate(refs):
        weights = n[i] + mm(z[:, sl(nb, nb + 1)], x)
        y_ref[sl(i, i + 1), :] = z[:, sl(1, nb)] - mm(z[:, sl(0, 1)], weights)


def quad_kernel(
    nb, place_ref, zs0, zs1, zs2, zs3, y01, y23,
    out_ref, send_ref, own_ref, z, y, act_ref, x_scr, r_scr, sem,
):
    copies = [
        pltpu.make_async_copy(y01, y.at[pl.ds(0, 2 * B), pl.ds(B, (nb - 1) * B)], sem.at[4]),
        pltpu.make_async_copy(y23, y.at[pl.ds(2 * B, 2 * B), pl.ds(B, (nb - 1) * B)], sem.at[5]),
    ] + [
        pltpu.make_async_copy(
            src.at[:, pl.ds(B, (nb - 1) * B)],
            z.at[pl.ds(i * B, B), pl.ds(B, (nb - 1) * B)],
            sem.at[i],
        )
        for i, src in enumerate((zs0, zs1, zs2, zs3))
    ]
    for copy in copies:
        copy.start()
    for copy in copies:
        copy.wait()
    rows = [slice(0, 2 * B), slice(2 * B, 4 * B)]
    m = [tn(z[rows[n], sl(1, 2)], y[rows[n], sl(1, nb)]) for n in range(2)]
    s = unit_inverse([m[n][:, :B] for n in range(2)], x_scr, r_scr)
    nn = [mm(s[n], m[n][:, B:]) for n in range(2)]
    x = mm(pair_inverse(s[0], s[1]), nn[0] + nn[1])
    last = nb - 1
    for n in range(2):
        weights = nn[n] + mm(s[n], x)
        y[rows[n], sl(2, nb)] = y[rows[n], sl(2, nb)] - mm(y[rows[n], sl(1, 2)], weights)
    m2 = tn(z[:, sl(2, 3)], y[:, sl(2, nb)])
    (s2,) = unit_inverse([m2[:, :B]], x_scr, r_scr)
    n2 = mm(s2, m2[:, B:])
    m3 = tn(z[:, sl(3, 4)], y[:, sl(3, nb)]) - tn(m2[:, sl(1, 2)], n2)
    wide = nb - 3
    act_ref[:, sl(0, 1)] = s2
    act_ref[:, sl(1, 1 + wide)] = n2
    act_ref[:, sl(1 + wide, 1 + 2 * wide)] = m3
    y2 = y[0:B, sl(2, 3)]
    own_ref[:, sl(1, nb - 2)] = y[0:B, sl(3, nb)] - mm(y2, n2)
    own_ref[:, sl(0, 1)] = mm(y2, s2)

    at = 1 + 2 * wide
    for a in range(4, last):
        act_ref[:, sl(at, at + nb - a)] = tn(z[:, sl(a, a + 1)], y[:, sl(a, nb)]) - tn(
            m2[:, sl(a - 2, a - 1)], n2[:, sl(a - 3, wide)]
        )
        at += nb - a
    rows = pl.ds(pl.multiple_of(place_ref[0] * (B // 4), B // 4), B // 4)
    head, half = cuts(nb)
    out_ref[:, sl(0, head)] = act_ref[rows, sl(0, head)]
    first = sl(head, head + half)
    second = sl(head + half, head + 2 * half)

    @pl.when(place_ref[1] == 0)
    def _():
        out_ref[:, first] = act_ref[rows, first]
        send_ref[...] = act_ref[rows, second]

    @pl.when(place_ref[1] == 1)
    def _():
        out_ref[:, first] = act_ref[rows, second]
        send_ref[...] = act_ref[rows, first]


def cuts(nb):
    rest = sum(nb - a for a in range(5, nb - 1))
    return 1 + 2 * (nb - 3) + nb - 4, rest // 2


def ring_kernel(
    nb, side_ref, all_ref, own_ref, pay_ref, out_ref,
    act_ref, pas_ref, la, lb, q, m, nn, tot, x_scr, r_scr, s_scr, sem,
):
    wide = nb - 3
    deep = nb - 4
    active = 1 + 2 * wide
    copies = [
        pltpu.make_async_copy(all_ref.at[:, pl.ds(0, active * B)], act_ref, sem.at[0]),
        pltpu.make_async_copy(
            all_ref.at[:, pl.ds(active * B, pas_ref.shape[1])], pas_ref, sem.at[1]
        ),
    ]
    for copy in copies:
        copy.start()
    copies[0].wait()

    def piece(group, k):
        return act_ref[sl(group, group + 1), sl(k, k + 1)]

    for node in range(2):
        g, h = 2 * node, 2 * node + 1
        for k in range(wide):
            q[node, :, sl(k, k + 1)] = piece(g, 1 + k) + piece(h, 1 + k)
        t = pair_inverse(piece(g, 0), piece(h, 0))
        x = mm(t, q[node])
        m[node] = x
        lb[sl(node, node + 1), :] = x[:, B:]
        la[sl(node, node + 1), :] = q[node, :, B:]
        m3 = tn(q[node, :, :B], x)
        for k in range(wide):
            nn[node, :, sl(k, k + 1)] = (
                piece(g, 1 + wide + k) + piece(h, 1 + wide + k) - m3[:, sl(k, k + 1)]
            )
    s = unit_inverse([nn[0, :, :B], nn[1, :, :B]], x_scr, r_scr)
    for node in range(2):
        s_scr[node] = s[node]
        la[sl(2 + node, 3 + node), :] = nn[node, :, B:]
        lb[sl(2 + node, 3 + node), :] = mm(s[node], nn[node, :, B:])
    q3 = lb[sl(2, 3), :] + lb[sl(3, 4), :]
    x3 = mm(pair_inverse(s[0], s[1]), q3)
    la[sl(4, 5), :] = q3
    lb[sl(4, 5), :] = x3
    copies[1].wait()
    half = cuts(nb)[1]
    tot[...] = jnp.zeros_like(tot)

    def over(part):
        return (
            pas_ref[sl(0, 1), part]
            + pas_ref[sl(1, 2), part]
            + pas_ref[sl(2, 3), part]
            + pas_ref[sl(3, 4), part]
        )

    tot[:, sl(0, deep)] = over(sl(0, deep))
    lanes = pl.ds(pl.multiple_of((deep + half * side_ref[1]) * B, B), half * B)
    tot[:, lanes] = over(sl(deep, deep + half))
    at = 0
    for k in range(deep - 1):
        part = sl(at, at + deep - k)
        tot[:, part] = tot[:, part] - tn(la[:, sl(k, k + 1)], lb[:, sl(k, deep)])
        at += deep - k

    def panel(a):
        at = sum(nb - k for k in range(4, a))
        return tot[:, sl(at, at + nb - a)]

    own_side(nb, 4, panel, pay_ref, x_scr, r_scr)
    side = side_ref[0]
    y = own_ref[:, sl(1, nb - 2)] - mm(own_ref[:, :B], m[side])
    n3 = lb[pl.ds(pl.multiple_of((2 + side) * B, B), B), :]
    weights = n3 + mm(s_scr[side], x3)
    out_ref[...] = y[:, B:] - mm(y[:, :B], weights)


def own_side(nb, level, m, pay_ref, x_scr, r_scr):
    row = m(level)
    wide = nb - 1 - level
    (s,) = unit_inverse([row[:, :B]], x_scr, r_scr)
    n = mm(s, row[:, B:])
    pay_ref[:, sl(0, 1)] = s
    pay_ref[:, sl(1, 1 + wide)] = n
    at = 1 + wide
    for a in range(level + 1, nb - 1):
        k = a - level
        pay_ref[:, sl(at, at + nb - a)] = m(a) - tn(
            row[:, sl(k, k + 1)], n[:, sl(k - 1, wide)]
        )
        at += nb - a


def merge_kernel(nb, level, split, core_ref, own_ref, *refs):
    refs = list(refs)
    if split:
        kept, fetched = refs[:2]
        full, core = refs[-1], core_ref[0]
        full[core] = kept[...]
        full[1 - core] = fetched[...]
        other = functools.partial(two_part, full, full.shape[2] // B)
        refs = refs[3:-1]
    else:
        whole = refs[0]
        other = lambda i, j: whole[:, sl(i, j)]
        refs = refs[2:]
    after = refs[2:-2]
    pay_ref, x_ref = refs[:2]
    x_scr, r_scr = refs[-2:]
    wide = nb - 1 - level
    q = own_ref[:, sl(1, 1 + wide)] + other(1, 1 + wide)
    x = mm(pair_inverse(own_ref[:, :B], other(0, 1)), q)
    x_ref[...] = x

    def panel(a):
        k = a - level - 1
        at = 1 + wide + sum(nb - j for j in range(level + 1, a))
        return (
            own_ref[:, sl(at, at + nb - a)]
            + other(at, at + nb - a)
            - tn(q[:, sl(k, k + 1)], x[:, sl(k, wide)])
        )

    own_side(nb, level + 1, panel, pay_ref, x_scr, r_scr)
    if after:
        put_half(core_ref, pay_ref, after[0])


def two_part(full, half, i, j):
    if j <= half:
        return full[0, :, sl(i, j)]
    if i >= half:
        return full[1, :, sl(i - half, j - half)]
    return jnp.concatenate([full[0, :, sl(i, half)], full[1, :, sl(0, j - half)]], axis=1)


def put_half(core_ref, pay_ref, half_ref):
    count, half = pay_ref.shape[1] // B, half_ref.shape[1] // B

    @pl.when(core_ref[0] == 0)
    def _():
        half_ref[...] = pay_ref[:, sl(0, half)]

    @pl.when(core_ref[0] == 1)
    def _():
        half_ref[:, sl(0, count - half)] = pay_ref[:, sl(half, count)]
        if 2 * half > count:
            half_ref[:, sl(count - half, half)] = pay_ref[:, sl(count - 1, count)]


def update_kernel(pay_ref, x_ref, y_ref, out_ref):
    wide = x_ref.shape[1]
    weights = pay_ref[:, B : B + wide] + mm(pay_ref[:, :B], x_ref[...])
    out_ref[...] = y_ref[:, B:] - mm(y_ref[:, :B], weights)


def finish_kernel(order_ref, r_ref, own_ref, other_ref, y_ref, out_ref):
    s = own_ref[:, :B]
    n = own_ref[:, B:]
    x = mm(pair_inverse(s, other_ref[:, :B]), n + other_ref[:, B:])
    y = y_ref[:, B:] - mm(y_ref[:, :B], n + mm(s, x))
    pick = (lax.broadcasted_iota(jnp.int32, (B, B), 0) == order_ref[...]).astype(F32)
    out_ref[...] = exact(pick, tn(r_ref[...], y))


def call(kernel, shapes, args, scratch=(), in_specs=None, grid=(), interpret=False):
    shapes = [
        jax.ShapeDtypeStruct((B, w * B) if isinstance(w, int) else w, F32) for w in shapes
    ]
    vmem = pl.BlockSpec(memory_space=pltpu.VMEM)
    one = len(shapes) == 1
    return pl.pallas_call(
        kernel,
        out_shape=shapes[0] if one else shapes,
        grid=grid,
        in_specs=[vmem] * len(args) if in_specs is None else in_specs,
        out_specs=vmem if one else [vmem] * len(shapes),
        scratch_shapes=list(scratch),
        interpret=interpret,
    )(*args)


def swapped(block, axis, bit):
    count = lax.axis_size(axis)
    return lax.ppermute(block, axis, [(k, k ^ (1 << bit)) for k in range(count)])


def pay_width(levels, level):
    return 1 + (levels - level) + sum(levels + 1 - a for a in range(level + 1, levels))


def ring_call(run, levels, side, gathered, own):
    nb = levels + 1
    head, half = cuts(nb)
    active = 2 * levels - 3
    two = [pltpu.VMEM((2, B, B), F32)] * 2
    smem = pl.BlockSpec(memory_space=pltpu.SMEM)
    vmem = pl.BlockSpec(memory_space=pltpu.VMEM)
    anywhere = pl.BlockSpec(memory_space=pl.ANY)
    return run(
        functools.partial(ring_kernel, nb),
        [pay_width(levels, 4), nb - 4],
        [side, gathered, own],
        [
            pltpu.VMEM((4 * B, active * B), F32),
            pltpu.VMEM((4 * B, (head + half - active) * B), F32),
            pltpu.VMEM((5 * B, (nb - 4) * B), F32),
            pltpu.VMEM((5 * B, (nb - 4) * B), F32),
            pltpu.VMEM((2, B, (nb - 3) * B), F32),
            pltpu.VMEM((2, B, (nb - 3) * B), F32),
            pltpu.VMEM((2, B, (nb - 3) * B), F32),
            pltpu.VMEM((B, (nb - 4 + 2 * half) * B), F32),
            *two,
            pltpu.VMEM((2, B, B), F32),
            pltpu.SemaphoreType.DMA((2,)),
        ],
        [smem, anywhere, vmem],
    )


def quad_call(run, levels, place, zs, ys):
    nb = levels + 1
    head, half = cuts(nb)
    two = [pltpu.VMEM((2, B, B), F32)] * 2
    smem = pl.BlockSpec(memory_space=pltpu.SMEM)
    anywhere = pl.BlockSpec(memory_space=pl.ANY)
    return run(
        functools.partial(quad_kernel, nb),
        [(B // 4, (head + half) * B), (B // 4, half * B), nb - 2],
        [place, *zs, *ys],
        [
            pltpu.VMEM((4 * B, nb * B), F32),
            pltpu.VMEM((4 * B, nb * B), F32),
            pltpu.VMEM((B, (head + 2 * half) * B), F32),
            *two,
            pltpu.SemaphoreType.DMA((6,)),
        ],
        [smem] + [anywhere] * 6,
    )


def merge_call(run, levels, level, core, pay, others, behind, half):
    nb = levels + 1
    split = len(others) == 2
    two = [pltpu.VMEM((2, B, B), F32)] * 2
    smem = pl.BlockSpec(memory_space=pltpu.SMEM)
    vmem = pl.BlockSpec(memory_space=pltpu.VMEM)
    anywhere = pl.BlockSpec(memory_space=pl.ANY)
    return run(
        functools.partial(merge_kernel, nb, level, split),
        [pay_width(levels, level + 1), levels - level] + ([half] if half else []),
        [core, pay, *others, behind],
        two + ([pltpu.VMEM((2, *others[0].shape), F32)] if split else []),
        [smem] + [vmem] * (1 + len(others)) + [anywhere],
    )


def body(right_sides, leaf_order, leaf_inverse, basis_blocks, interpret=False):
    run = functools.partial(call, interpret=interpret)
    part = functools.partial
    levels = basis_blocks.shape[0]
    nb = levels + 1
    two = [pltpu.VMEM((2, B, B), F32)] * 2
    vmem = pl.BlockSpec(memory_space=pltpu.VMEM)

    z0 = run(part(leaf_kernel, nb), [nb + 1], [leaf_order, leaf_inverse, basis_blocks, right_sides], two)
    z1 = swapped(z0, "inner", 0)
    z2 = swapped(z0, "inner", 1)
    z3 = swapped(z2, "inner", 0)
    ys = [
        run(part(pair_kernel, nb), [(2 * B, (nb - 1) * B)], pair) for pair in ((z0, z1), (z2, z3))
    ]
    place = lax.axis_index("inner").astype(jnp.int32)
    core = lax.axis_index("outer").astype(jnp.int32) & 1
    mine, send, own = quad_call(run, levels, jnp.stack([place & 3, core]), [z0, z1, z2, z3], ys)
    cut = cuts(nb)[0] * B
    mine = jnp.concatenate([mine[:, :cut], mine[:, cut:] + swapped(send, "outer", 0)], axis=1)
    gathered = lax.all_gather(mine, "inner", tiled=True)
    pay, y = ring_call(run, levels, jnp.stack([place >> 3, core]), gathered, own)
    core = core.reshape(1)
    half = None
    for level in range(4, levels):
        if half is None:
            others = [swapped(pay, "outer", level - 4)]
        else:
            kept = swapped(half, "outer", level - 4)
            others = [kept, swapped(kept, "outer", 0)]
        if level == levels - 1:
            break
        width = pay_width(levels, level + 1)
        cut = -(-width // 2) if width > 6 else 0
        found = merge_call(run, levels, level, core, pay, others, y, cut)
        wide = levels - level
        head = pl.BlockSpec((B, (1 + wide) * B), lambda i: (0, 0))
        y = run(update_kernel, [wide], [pay, found[1], y], (), [head, vmem, vmem], (1,))
        pay = found[0]
        half = found[2] if cut else None
    return run(finish_kernel, [1], [leaf_order, leaf_inverse, pay, others[0], y])


def solution(mesh):
    in_specs = (
        P(("outer", "inner"), None),
        P(("outer", "inner"), None),
        P(("outer", "inner"), None),
        P(None, ("outer", "inner"), None),
    )
    out_specs = P(("outer", "inner"), None)
    return jax.shard_map(body, mesh=mesh, in_specs=in_specs, out_specs=out_specs, check_vma=False)
```

```python
import functools

import jax
import jax.numpy as jnp
from jax import lax
from jax.experimental import pallas as pl
from jax.experimental.pallas import tpu as pltpu
from jax.sharding import PartitionSpec as P

B = 128
F32 = jnp.float32


HIGH = lax.Precision.HIGHEST
HALF = jnp.bfloat16


def product(a, b, axis):
    a_top, b_top = a.astype(HALF), b.astype(HALF)
    a_low = (a - a_top.astype(F32)).astype(HALF)
    b_low = (b - b_top.astype(F32)).astype(HALF)
    left = jnp.concatenate([a_top, a_low, a_top], axis=axis)
    right = jnp.concatenate([b_top, b_top, b_low], axis=0)
    return lax.dot_general(left, right, (((axis,), (0,)), ((), ())), preferred_element_type=F32)


def mm(a, b):
    return product(a, b, 1)


def tn(a, b):
    return product(a, b, 0)


def exact(a, b):
    return jnp.dot(a, b, precision=HIGH, preferred_element_type=F32)


def exact_tn(a, b):
    return lax.dot_general(
        a, b, (((0,), (0,)), ((), ())), precision=HIGH, preferred_element_type=F32
    )


def eye():
    return (
        lax.broadcasted_iota(jnp.int32, (B, B), 0) == lax.broadcasted_iota(jnp.int32, (B, B), 1)
    ).astype(F32)


def sl(i, j):
    return slice(i * B, j * B)


def unit_inverse(grams, x_ref, r_ref):
    unit = eye()
    count = len(grams)
    h = jnp.ones((1, 1), F32)
    for g in grams:
        h = jnp.maximum(
            h, jnp.max(jnp.sum(jnp.abs(g), axis=0, keepdims=True), axis=1, keepdims=True)
        )
    s = 2.0 / h
    s = 2.0 * s * (s + 2.0)
    left = jnp.zeros((1, 1), jnp.int32)
    ahead = s
    for _ in range(14):
        left = left + (ahead < 4000.0).astype(jnp.int32)
        ahead = 2.0 * ahead * (ahead + 2.0)
    steps = jnp.max(left)
    inv_t = 1.0 / (1.0 + s)
    c = 1.0 + inv_t
    scale = 2.0 / (h + 2.0)
    for k, g in enumerate(grams):
        r = (h * unit - 2.0 * g) / (h + 2.0)
        x_ref[k] = (c * scale) * (unit + r)
        r_ref[k] = c * mm(r, r) - inv_t * unit

    def double(_, s):
        s = 2.0 * s * (s + 2.0)
        inv_t = 1.0 / (1.0 + s)
        c = 1.0 + inv_t
        for k in range(count):
            r = r_ref[k]
            x = x_ref[k]
            x_ref[k] = c * (x + mm(x, r))
            r_ref[k] = c * mm(r, r) - inv_t * unit
        return s

    lax.fori_loop(0, steps, double, s)
    found = []
    for k, g in enumerate(grams):
        x = x_ref[k]
        found.append(x + mm(x, unit - x - exact(g, x)))
    return found


def pair_inverse(s_sum):
    unit = eye()
    r = 0.5 * (s_sum - unit)
    t = 7.0
    x = (0.5 * (1.0 + 1.0 / t)) * (unit + r)
    r = (1.0 + 1.0 / t) * mm(r, r) - (1.0 / t) * unit
    for last in (False, False, True):
        t = 2.0 * t * t - 1.0
        c = 1.0 + 1.0 / t
        x = c * (x + mm(x, r))
        if not last:
            r = c * mm(r, r) - (1.0 / t) * unit
    return x


def leaf_kernel(nb, order_ref, r_ref, u_ref, rhs_ref, z_ref, x_scr, r_scr):
    pick = (lax.broadcasted_iota(jnp.int32, (B, B), 0) == order_ref[...]).astype(F32)
    r = r_ref[...]
    for b in range(nb - 1):
        z_ref[:, sl(b, b + 1)] = mm(r, u_ref[b])
    z_ref[:, sl(nb - 1, nb)] = mm(r, exact_tn(pick, rhs_ref[...]))
    z0 = z_ref[:, sl(0, 1)]
    (s,) = unit_inverse([tn(z0, z0)], x_scr, r_scr)
    z_ref[:, sl(nb, nb + 1)] = s


def pair_kernel(nb, first_ref, second_ref, y_ref):
    refs = (first_ref, second_ref)
    n = [
        exact(z[:, sl(nb, nb + 1)], tn(z[:, sl(0, 1)], z[:, sl(1, nb)]))
        for z in refs
    ]
    t = pair_inverse(first_ref[:, sl(nb, nb + 1)] + second_ref[:, sl(nb, nb + 1)])
    x = mm(t, n[0] + n[1])
    for i, z in enumerate(refs):
        weights = n[i] + mm(z[:, sl(nb, nb + 1)], x)
        y_ref[sl(i, i + 1), :] = z[:, sl(1, nb)] - mm(z[:, sl(0, 1)], weights)


def quad_kernel(
    nb, place_ref, zs0, zs1, zs2, zs3, y01, y23,
    out_ref, send_ref, own_ref, z, y, act_ref, x_scr, r_scr, sem,
):
    copies = [
        pltpu.make_async_copy(y01, y.at[pl.ds(0, 2 * B), pl.ds(B, (nb - 1) * B)], sem.at[4]),
        pltpu.make_async_copy(y23, y.at[pl.ds(2 * B, 2 * B), pl.ds(B, (nb - 1) * B)], sem.at[5]),
    ] + [
        pltpu.make_async_copy(
            src.at[:, pl.ds(B, (nb - 1) * B)],
            z.at[pl.ds(i * B, B), pl.ds(B, (nb - 1) * B)],
            sem.at[i],
        )
        for i, src in enumerate((zs0, zs1, zs2, zs3))
    ]
    for copy in copies:
        copy.start()
    for copy in copies:
        copy.wait()
    rows = [slice(0, 2 * B), slice(2 * B, 4 * B)]
    m = [tn(z[rows[n], sl(1, 2)], y[rows[n], sl(1, nb)]) for n in range(2)]
    s = unit_inverse([m[n][:, :B] for n in range(2)], x_scr, r_scr)
    nn = [mm(s[n], m[n][:, B:]) for n in range(2)]
    x = mm(pair_inverse(s[0] + s[1]), nn[0] + nn[1])
    last = nb - 1
    for n in range(2):
        weights = nn[n] + mm(s[n], x)
        y[rows[n], sl(2, nb)] = y[rows[n], sl(2, nb)] - mm(y[rows[n], sl(1, 2)], weights)
    m2 = tn(z[:, sl(2, 3)], y[:, sl(2, nb)])
    (s2,) = unit_inverse([m2[:, :B]], x_scr, r_scr)
    n2 = mm(s2, m2[:, B:])
    m3 = tn(z[:, sl(3, 4)], y[:, sl(3, nb)]) - tn(m2[:, sl(1, 2)], n2)
    wide = nb - 3
    act_ref[:, sl(0, 1)] = s2
    act_ref[:, sl(1, 1 + wide)] = n2
    act_ref[:, sl(1 + wide, 1 + 2 * wide)] = m3
    y2 = y[0:B, sl(2, 3)]
    own_ref[:, sl(1, nb - 2)] = y[0:B, sl(3, nb)] - mm(y2, n2)
    own_ref[:, sl(0, 1)] = mm(y2, s2)

    at = 1 + 2 * wide
    for a in range(4, last):
        act_ref[:, sl(at, at + nb - a)] = tn(z[:, sl(a, a + 1)], y[:, sl(a, nb)]) - tn(
            m2[:, sl(a - 2, a - 1)], n2[:, sl(a - 3, wide)]
        )
        at += nb - a
    head, half = cuts(nb)
    first = sl(head, head + half)
    second = sl(head + half, head + 2 * half)
    for part in range(2):
        rows = pl.ds(pl.multiple_of(part * (B // 2) + place_ref[0] * SHARE, SHARE), SHARE)
        put = slice(part * SHARE, (part + 1) * SHARE)
        out_ref[put, sl(0, head)] = act_ref[rows, sl(0, head)]

        @pl.when(place_ref[1] == 0)
        def _():
            out_ref[put, first] = act_ref[rows, first]
            send_ref[put, :] = act_ref[rows, second]

        @pl.when(place_ref[1] == 1)
        def _():
            out_ref[put, first] = act_ref[rows, second]
            send_ref[put, :] = act_ref[rows, first]


SHARE = B // 8


def halve_kernel(cut, bit_ref, out_ref, got_ref, keep_ref, give_ref):
    bit = bit_ref[0]
    for to, at in ((keep_ref, bit), (give_ref, 1 - bit)):
        rows = pl.ds(pl.multiple_of(at * SHARE, SHARE), SHARE)
        to[:, :cut] = out_ref[rows, :cut]
        to[:, cut:] = out_ref[rows, cut:] + got_ref[rows, :]


def cuts(nb):
    rest = sum(nb - a for a in range(5, nb - 1))
    return 1 + 2 * (nb - 3) + nb - 4, rest // 2


def ring_kernel(
    nb, side_ref, all_ref, own_ref, pay_ref, out_ref,
    act_ref, pas_ref, la, lb, m, nn, tot, x_scr, r_scr, s_scr, sem,
):
    wide = nb - 3
    deep = nb - 4
    active = 1 + 2 * wide
    copies = [
        pltpu.make_async_copy(all_ref.at[:, pl.ds(0, active * B)], act_ref, sem.at[0]),
        pltpu.make_async_copy(
            all_ref.at[:, pl.ds(active * B, pas_ref.shape[1])], pas_ref, sem.at[1]
        ),
    ]
    for copy in copies:
        copy.start()
    copies[0].wait()

    for node in range(2):
        rows = sl(node, node + 1)
        q = act_ref[rows, sl(1, 1 + wide)]
        x = mm(pair_inverse(act_ref[rows, :B]), q)
        m[node] = x
        lb[rows, :] = x[:, B:]
        la[rows, :] = q[:, B:]
        nn[node] = act_ref[rows, sl(1 + wide, active)] - tn(q[:, :B], x)
    s = unit_inverse([nn[0, :, :B], nn[1, :, :B]], x_scr, r_scr)
    for node in range(2):
        s_scr[node] = s[node]
        la[sl(2 + node, 3 + node), :] = nn[node, :, B:]
        lb[sl(2 + node, 3 + node), :] = mm(s[node], nn[node, :, B:])
    q3 = lb[sl(2, 3), :] + lb[sl(3, 4), :]
    x3 = mm(pair_inverse(s[0] + s[1]), q3)
    la[sl(4, 5), :] = q3
    lb[sl(4, 5), :] = x3
    copies[1].wait()
    half = cuts(nb)[1]
    tot[...] = jnp.zeros_like(tot)

    def over(part):
        return pas_ref[sl(0, 1), part] + pas_ref[sl(1, 2), part]

    tot[:, sl(0, deep)] = over(sl(0, deep))
    lanes = pl.ds(pl.multiple_of((deep + half * side_ref[1]) * B, B), half * B)
    tot[:, lanes] = over(sl(deep, deep + half))
    at = 0
    for k in range(deep - 1):
        part = sl(at, at + deep - k)
        tot[:, part] = tot[:, part] - tn(la[:, sl(k, k + 1)], lb[:, sl(k, deep)])
        at += deep - k

    def panel(a):
        at = sum(nb - k for k in range(4, a))
        return tot[:, sl(at, at + nb - a)]

    own_side(nb, 4, panel, pay_ref, x_scr, r_scr)
    side = side_ref[0]
    y = own_ref[:, sl(1, nb - 2)] - mm(own_ref[:, :B], m[side])
    n3 = lb[pl.ds(pl.multiple_of((2 + side) * B, B), B), :]
    weights = n3 + mm(s_scr[side], x3)
    out_ref[...] = y[:, B:] - mm(y[:, :B], weights)


def own_side(nb, level, m, pay_ref, x_scr, r_scr):
    row = m(level)
    wide = nb - 1 - level
    (s,) = unit_inverse([row[:, :B]], x_scr, r_scr)
    n = mm(s, row[:, B:])
    pay_ref[:, sl(0, 1)] = s
    pay_ref[:, sl(1, 1 + wide)] = n
    at = 1 + wide
    for a in range(level + 1, nb - 1):
        k = a - level
        pay_ref[:, sl(at, at + nb - a)] = m(a) - tn(
            row[:, sl(k, k + 1)], n[:, sl(k - 1, wide)]
        )
        at += nb - a


def merge_kernel(nb, level, split, core_ref, own_ref, *refs):
    refs = list(refs)
    if split:
        kept, fetched = refs[:2]
        full, core = refs[-1], core_ref[0]
        full[core] = kept[...]
        full[1 - core] = fetched[...]
        other = functools.partial(two_part, full, full.shape[2] // B)
        refs = refs[3:-1]
    else:
        whole = refs[0]
        other = lambda i, j: whole[:, sl(i, j)]
        refs = refs[2:]
    after = refs[2:-2]
    pay_ref, x_ref = refs[:2]
    x_scr, r_scr = refs[-2:]
    wide = nb - 1 - level
    q = own_ref[:, sl(1, 1 + wide)] + other(1, 1 + wide)
    x = mm(pair_inverse(own_ref[:, :B] + other(0, 1)), q)
    x_ref[...] = x

    def panel(a):
        k = a - level - 1
        at = 1 + wide + sum(nb - j for j in range(level + 1, a))
        return (
            own_ref[:, sl(at, at + nb - a)]
            + other(at, at + nb - a)
            - tn(q[:, sl(k, k + 1)], x[:, sl(k, wide)])
        )

    own_side(nb, level + 1, panel, pay_ref, x_scr, r_scr)
    if after:
        put_half(core_ref, pay_ref, after[0])


def two_part(full, half, i, j):
    if j <= half:
        return full[0, :, sl(i, j)]
    if i >= half:
        return full[1, :, sl(i - half, j - half)]
    return jnp.concatenate([full[0, :, sl(i, half)], full[1, :, sl(0, j - half)]], axis=1)


def put_half(core_ref, pay_ref, half_ref):
    count, half = pay_ref.shape[1] // B, half_ref.shape[1] // B

    @pl.when(core_ref[0] == 0)
    def _():
        half_ref[...] = pay_ref[:, sl(0, half)]

    @pl.when(core_ref[0] == 1)
    def _():
        half_ref[:, sl(0, count - half)] = pay_ref[:, sl(half, count)]
        if 2 * half > count:
            half_ref[:, sl(count - half, half)] = pay_ref[:, sl(count - 1, count)]


def update_kernel(pay_ref, x_ref, y_ref, out_ref):
    wide = x_ref.shape[1]
    weights = pay_ref[:, B : B + wide] + mm(pay_ref[:, :B], x_ref[...])
    out_ref[...] = y_ref[:, B:] - mm(y_ref[:, :B], weights)


def finish_kernel(order_ref, r_ref, own_ref, other_ref, y_ref, out_ref):
    s = own_ref[:, :B]
    n = own_ref[:, B:]
    x = mm(pair_inverse(s + other_ref[:, :B]), n + other_ref[:, B:])
    y = y_ref[:, B:] - mm(y_ref[:, :B], n + mm(s, x))
    pick = (lax.broadcasted_iota(jnp.int32, (B, B), 0) == order_ref[...]).astype(F32)
    out_ref[...] = exact(pick, tn(r_ref[...], y))


def call(kernel, shapes, args, scratch=(), in_specs=None, grid=(), interpret=False):
    shapes = [
        jax.ShapeDtypeStruct((B, w * B) if isinstance(w, int) else w, F32) for w in shapes
    ]
    vmem = pl.BlockSpec(memory_space=pltpu.VMEM)
    one = len(shapes) == 1
    return pl.pallas_call(
        kernel,
        out_shape=shapes[0] if one else shapes,
        grid=grid,
        in_specs=[vmem] * len(args) if in_specs is None else in_specs,
        out_specs=vmem if one else [vmem] * len(shapes),
        scratch_shapes=list(scratch),
        interpret=interpret,
    )(*args)


def swapped(block, axis, bit):
    count = lax.axis_size(axis)
    return lax.ppermute(block, axis, [(k, k ^ (1 << bit)) for k in range(count)])


def pay_width(levels, level):
    return 1 + (levels - level) + sum(levels + 1 - a for a in range(level + 1, levels))


def ring_call(run, levels, side, gathered, own):
    nb = levels + 1
    head, half = cuts(nb)
    active = 2 * levels - 3
    two = [pltpu.VMEM((2, B, B), F32)] * 2
    smem = pl.BlockSpec(memory_space=pltpu.SMEM)
    vmem = pl.BlockSpec(memory_space=pltpu.VMEM)
    anywhere = pl.BlockSpec(memory_space=pl.ANY)
    return run(
        functools.partial(ring_kernel, nb),
        [pay_width(levels, 4), nb - 4],
        [side, gathered, own],
        [
            pltpu.VMEM((2 * B, active * B), F32),
            pltpu.VMEM((2 * B, (head + half - active) * B), F32),
            pltpu.VMEM((5 * B, (nb - 4) * B), F32),
            pltpu.VMEM((5 * B, (nb - 4) * B), F32),
            pltpu.VMEM((2, B, (nb - 3) * B), F32),
            pltpu.VMEM((2, B, (nb - 3) * B), F32),
            pltpu.VMEM((B, (nb - 4 + 2 * half) * B), F32),
            *two,
            pltpu.VMEM((2, B, B), F32),
            pltpu.SemaphoreType.DMA((2,)),
        ],
        [smem, anywhere, vmem],
    )


def quad_call(run, levels, place, zs, ys):
    nb = levels + 1
    head, half = cuts(nb)
    two = [pltpu.VMEM((2, B, B), F32)] * 2
    smem = pl.BlockSpec(memory_space=pltpu.SMEM)
    anywhere = pl.BlockSpec(memory_space=pl.ANY)
    return run(
        functools.partial(quad_kernel, nb),
        [(2 * SHARE, (head + half) * B), (2 * SHARE, half * B), nb - 2],
        [place, *zs, *ys],
        [
            pltpu.VMEM((4 * B, nb * B), F32),
            pltpu.VMEM((4 * B, nb * B), F32),
            pltpu.VMEM((B, (head + 2 * half) * B), F32),
            *two,
            pltpu.SemaphoreType.DMA((6,)),
        ],
        [smem] + [anywhere] * 6,
    )


def near(x):
    return pltpu.with_memory_space_constraint(x, pltpu.VMEM)


def merge_call(run, levels, level, core, pay, others, behind, half):
    nb = levels + 1
    split = len(others) == 2
    two = [pltpu.VMEM((2, B, B), F32)] * 2
    smem = pl.BlockSpec(memory_space=pltpu.SMEM)
    vmem = pl.BlockSpec(memory_space=pltpu.VMEM)
    anywhere = pl.BlockSpec(memory_space=pl.ANY)
    return run(
        functools.partial(merge_kernel, nb, level, split),
        [pay_width(levels, level + 1), levels - level] + ([half] if half else []),
        [core, pay, *[near(o) for o in others], behind],
        two + ([pltpu.VMEM((2, *others[0].shape), F32)] if split else []),
        [smem] + [vmem] * (1 + len(others)) + [anywhere],
    )


def body(right_sides, leaf_order, leaf_inverse, basis_blocks, interpret=False):
    run = functools.partial(call, interpret=interpret)
    part = functools.partial
    levels = basis_blocks.shape[0]
    nb = levels + 1
    two = [pltpu.VMEM((2, B, B), F32)] * 2
    vmem = pl.BlockSpec(memory_space=pltpu.VMEM)

    z0 = run(part(leaf_kernel, nb), [nb + 1], [leaf_order, leaf_inverse, basis_blocks, right_sides], two)
    z1 = swapped(z0, "inner", 0)
    z2 = swapped(z0, "inner", 1)
    z3 = swapped(z2, "inner", 0)
    ys = [
        run(part(pair_kernel, nb), [(2 * B, (nb - 1) * B)], pair) for pair in ((z0, z1), (z2, z3))
    ]
    place = lax.axis_index("inner").astype(jnp.int32)
    core = lax.axis_index("outer").astype(jnp.int32) & 1
    mine, send, own = quad_call(run, levels, jnp.stack([place & 3, core]), [z0, z1, z2, z3], ys)
    cut = cuts(nb)[0] * B
    half = (SHARE, mine.shape[1])
    keep, give = run(
        part(halve_kernel, cut),
        [half, half],
        [(place >> 2 & 1).reshape(1), mine, near(swapped(send, "outer", 0))],
        (),
        [pl.BlockSpec(memory_space=pltpu.SMEM)] + [pl.BlockSpec(memory_space=pltpu.VMEM)] * 2,
    )
    mine = keep + swapped(give, "inner", 2)
    gathered = lax.all_gather(mine, "inner", tiled=True)
    pay, y = ring_call(run, levels, jnp.stack([place >> 3, core]), gathered, own)
    core = core.reshape(1)
    half = None
    for level in range(4, levels):
        if half is None:
            others = [swapped(pay, "outer", level - 4)]
        else:
            kept = swapped(half, "outer", level - 4)
            others = [kept, swapped(kept, "outer", 0)]
        if level == levels - 1:
            break
        width = pay_width(levels, level + 1)
        cut = -(-width // 2) if width > 6 else 0
        found = merge_call(run, levels, level, core, pay, others, y, cut)
        wide = levels - level
        head = pl.BlockSpec((B, (1 + wide) * B), lambda i: (0, 0))
        y = run(update_kernel, [wide], [pay, found[1], y], (), [head, vmem, vmem], (1,))
        pay = found[0]
        half = found[2] if cut else None
    return run(finish_kernel, [1], [leaf_order, leaf_inverse, pay, near(others[0]), y])


def solution(mesh):
    in_specs = (
        P(("outer", "inner"), None),
        P(("outer", "inner"), None),
        P(("outer", "inner"), None),
        P(None, ("outer", "inner"), None),
    )
    out_specs = P(("outer", "inner"), None)
    return jax.shard_map(body, mesh=mesh, in_specs=in_specs, out_specs=out_specs, check_vma=False)
```

```python
import functools

import jax
import jax.numpy as jnp
from jax import lax
from jax.experimental import pallas as pl
from jax.experimental.pallas import tpu as pltpu
from jax.sharding import PartitionSpec as P

B = 128
F32 = jnp.float32


HIGH = lax.Precision.HIGHEST
HALF = jnp.bfloat16


def product(a, b, axis):
    a_top, b_top = a.astype(HALF), b.astype(HALF)
    a_low = (a - a_top.astype(F32)).astype(HALF)
    b_low = (b - b_top.astype(F32)).astype(HALF)
    left = jnp.concatenate([a_top, a_low, a_top], axis=axis)
    right = jnp.concatenate([b_top, b_top, b_low], axis=0)
    return lax.dot_general(left, right, (((axis,), (0,)), ((), ())), preferred_element_type=F32)


def mm(a, b):
    return product(a, b, 1)


def tn(a, b):
    return product(a, b, 0)


def exact(a, b):
    return jnp.dot(a, b, precision=HIGH, preferred_element_type=F32)


def exact_tn(a, b):
    return lax.dot_general(
        a, b, (((0,), (0,)), ((), ())), precision=HIGH, preferred_element_type=F32
    )


def eye():
    return (
        lax.broadcasted_iota(jnp.int32, (B, B), 0) == lax.broadcasted_iota(jnp.int32, (B, B), 1)
    ).astype(F32)


def sl(i, j):
    return slice(i * B, j * B)


def unit_inverse(grams, x_ref, r_ref):
    unit = eye()
    count = len(grams)
    h = jnp.ones((1, 1), F32)
    for g in grams:
        h = jnp.maximum(
            h, jnp.max(jnp.sum(jnp.abs(g), axis=0, keepdims=True), axis=1, keepdims=True)
        )
    s = 2.0 / h
    s = 2.0 * s * (s + 2.0)
    left = jnp.zeros((1, 1), jnp.int32)
    ahead = s
    for _ in range(14):
        left = left + (ahead < 4000.0).astype(jnp.int32)
        ahead = 2.0 * ahead * (ahead + 2.0)
    steps = jnp.max(left)
    inv_t = 1.0 / (1.0 + s)
    c = 1.0 + inv_t
    scale = 2.0 / (h + 2.0)
    for k, g in enumerate(grams):
        r = (h * unit - 2.0 * g) / (h + 2.0)
        x_ref[k] = (c * scale) * (unit + r)
        r_ref[k] = c * mm(r, r) - inv_t * unit

    def double(_, s):
        s = 2.0 * s * (s + 2.0)
        inv_t = 1.0 / (1.0 + s)
        c = 1.0 + inv_t
        for k in range(count):
            r = r_ref[k]
            x = x_ref[k]
            x_ref[k] = c * (x + mm(x, r))
            r_ref[k] = c * mm(r, r) - inv_t * unit
        return s

    lax.fori_loop(0, steps, double, s)
    found = []
    for k, g in enumerate(grams):
        x = x_ref[k]
        found.append(x + mm(x, unit - x - exact(g, x)))
    return found


def pair_inverse(s_first, s_second):
    unit = eye()
    r = 0.5 * (s_first + s_second - unit)
    t = 7.0
    x = (0.5 * (1.0 + 1.0 / t)) * (unit + r)
    r = (1.0 + 1.0 / t) * mm(r, r) - (1.0 / t) * unit
    for last in (False, False, True):
        t = 2.0 * t * t - 1.0
        c = 1.0 + 1.0 / t
        x = c * (x + mm(x, r))
        if not last:
            r = c * mm(r, r) - (1.0 / t) * unit
    return x


def leaf_kernel(nb, order_ref, r_ref, u_ref, rhs_ref, z_ref):
    pick = (lax.broadcasted_iota(jnp.int32, (B, B), 0) == order_ref[...]).astype(F32)
    r = r_ref[...]
    for b in range(nb - 1):
        z_ref[:, sl(b, b + 1)] = mm(r, u_ref[b])
    z_ref[:, sl(nb - 1, nb)] = mm(r, exact_tn(pick, rhs_ref[...]))


def pair_level(nb, refs, s, n, y_ref):
    x = mm(pair_inverse(s[0], s[1]), n[0] + n[1])
    for i, z in enumerate(refs):
        weights = n[i] + mm(s[i], x)
        y_ref[sl(i, i + 1), :] = z[:, sl(1, nb)] - mm(z[:, sl(0, 1)], weights)


def near_kernel(nb, z0, z1, z2, y_ref, side_ref, x_scr, r_scr):
    refs = (z0, z1, z2)
    p = [tn(z[:, :B], z[...]) for z in refs]
    s = unit_inverse([a[:, :B] for a in p], x_scr, r_scr)
    n = [exact(s[i], p[i][:, B:]) for i in range(3)]
    side_ref[:, :B] = s[2]
    side_ref[:, B:] = n[2]
    pair_level(nb, refs[:2], s, n, y_ref)


def far_kernel(nb, z2, z3, side_ref, y_ref, x_scr, r_scr):
    p = tn(z3[:, :B], z3[...])
    (s,) = unit_inverse([p[:, :B]], x_scr, r_scr)
    n = exact(s, p[:, B:])
    pair_level(nb, (z2, z3), (side_ref[:, :B], s), (side_ref[:, B:], n), y_ref)


def quad_kernel(
    nb, place_ref, zs0, zs1, zs2, zs3, y01, y23,
    out_ref, keep_ref, send_ref, own_ref, z, y, act_ref, x_scr, r_scr, sem,
):
    copies = [
        pltpu.make_async_copy(y01, y.at[pl.ds(0, 2 * B), pl.ds(B, (nb - 1) * B)], sem.at[4]),
        pltpu.make_async_copy(y23, y.at[pl.ds(2 * B, 2 * B), pl.ds(B, (nb - 1) * B)], sem.at[5]),
    ] + [
        pltpu.make_async_copy(
            src.at[:, pl.ds(B, (nb - 1) * B)],
            z.at[pl.ds(i * B, B), pl.ds(B, (nb - 1) * B)],
            sem.at[i],
        )
        for i, src in enumerate((zs0, zs1, zs2, zs3))
    ]
    for copy in copies:
        copy.start()
    for copy in copies:
        copy.wait()
    rows = [slice(0, 2 * B), slice(2 * B, 4 * B)]
    m = [tn(z[rows[n], sl(1, 2)], y[rows[n], sl(1, nb)]) for n in range(2)]
    s = unit_inverse([m[n][:, :B] for n in range(2)], x_scr, r_scr)
    nn = [mm(s[n], m[n][:, B:]) for n in range(2)]
    x = mm(pair_inverse(s[0], s[1]), nn[0] + nn[1])
    last = nb - 1
    for n in range(2):
        weights = nn[n] + mm(s[n], x)
        y[rows[n], sl(2, nb)] = y[rows[n], sl(2, nb)] - mm(y[rows[n], sl(1, 2)], weights)
    m2 = tn(z[:, sl(2, 3)], y[:, sl(2, nb)])
    (s2,) = unit_inverse([m2[:, :B]], x_scr, r_scr)
    n2 = mm(s2, m2[:, B:])
    m3 = tn(z[:, sl(3, 4)], y[:, sl(3, nb)]) - tn(m2[:, sl(1, 2)], n2)
    wide = nb - 3
    act_ref[:, sl(0, 1)] = s2
    act_ref[:, sl(1, 1 + wide)] = n2
    act_ref[:, sl(1 + wide, 1 + 2 * wide)] = m3
    y2 = y[0:B, sl(2, 3)]
    own_ref[:, sl(1, nb - 2)] = y[0:B, sl(3, nb)] - mm(y2, n2)
    own_ref[:, sl(0, 1)] = mm(y2, s2)

    at = 1 + 2 * wide
    for a in range(4, last):
        act_ref[:, sl(at, at + nb - a)] = tn(z[:, sl(a, a + 1)], y[:, sl(a, nb)]) - tn(
            m2[:, sl(a - 2, a - 1)], n2[:, sl(a - 3, wide)]
        )
        at += nb - a
    rows = pl.ds(pl.multiple_of(place_ref[0] * (B // 4), B // 4), B // 4)
    head, half = cuts(nb)
    out_ref[...] = act_ref[rows, sl(0, head)]
    first = sl(head, head + half)
    second = sl(head + half, head + 2 * half)

    @pl.when(place_ref[1] == 0)
    def _():
        keep_ref[...] = act_ref[rows, first]
        send_ref[...] = act_ref[rows, second]

    @pl.when(place_ref[1] == 1)
    def _():
        keep_ref[...] = act_ref[rows, second]
        send_ref[...] = act_ref[rows, first]


def cuts(nb):
    rest = sum(nb - a for a in range(5, nb - 1))
    return 1 + 2 * (nb - 3) + nb - 4, rest // 2


def ring_kernel(
    nb, side_ref, all_ref, rest0, rest1, rest2, rest3, own_ref, pay_ref, out_ref,
    act_ref, pas_ref, la, lb, q, m, nn, tot, x_scr, r_scr, s_scr, sem,
):
    wide = nb - 3
    deep = nb - 4
    active = 1 + 2 * wide
    copies = [
        pltpu.make_async_copy(all_ref.at[:, pl.ds(0, active * B)], act_ref, sem.at[0]),
        pltpu.make_async_copy(
            all_ref.at[:, pl.ds(active * B, pas_ref.shape[1])], pas_ref, sem.at[1]
        ),
    ]
    for copy in copies:
        copy.start()
    copies[0].wait()

    def piece(group, k):
        return act_ref[sl(group, group + 1), sl(k, k + 1)]

    for node in range(2):
        g, h = 2 * node, 2 * node + 1
        for k in range(wide):
            q[node, :, sl(k, k + 1)] = piece(g, 1 + k) + piece(h, 1 + k)
        t = pair_inverse(piece(g, 0), piece(h, 0))
        x = mm(t, q[node])
        m[node] = x
        lb[sl(node, node + 1), :] = x[:, B:]
        la[sl(node, node + 1), :] = q[node, :, B:]
        m3 = tn(q[node, :, :B], x)
        for k in range(wide):
            nn[node, :, sl(k, k + 1)] = (
                piece(g, 1 + wide + k) + piece(h, 1 + wide + k) - m3[:, sl(k, k + 1)]
            )
    s = unit_inverse([nn[0, :, :B], nn[1, :, :B]], x_scr, r_scr)
    for node in range(2):
        s_scr[node] = s[node]
        la[sl(2 + node, 3 + node), :] = nn[node, :, B:]
        lb[sl(2 + node, 3 + node), :] = mm(s[node], nn[node, :, B:])
    q3 = lb[sl(2, 3), :] + lb[sl(3, 4), :]
    x3 = mm(pair_inverse(s[0], s[1]), q3)
    la[sl(4, 5), :] = q3
    lb[sl(4, 5), :] = x3
    copies[1].wait()
    half = cuts(nb)[1]
    tot[...] = jnp.zeros_like(tot)

    def over(part):
        return (
            pas_ref[sl(0, 1), part]
            + pas_ref[sl(1, 2), part]
            + pas_ref[sl(2, 3), part]
            + pas_ref[sl(3, 4), part]
        )

    tot[:, sl(0, deep)] = over(sl(0, deep))
    lanes = pl.ds(pl.multiple_of((deep + half * side_ref[1]) * B, B), half * B)
    for k, rest in enumerate((rest0, rest1, rest2, rest3)):
        rows = pl.ds(pl.multiple_of((side_ref[2] ^ k) * (B // 4), B // 4), B // 4)
        tot[rows, lanes] = rest[...]
    at = 0
    for k in range(deep - 1):
        part = sl(at, at + deep - k)
        tot[:, part] = tot[:, part] - tn(la[:, sl(k, k + 1)], lb[:, sl(k, deep)])
        at += deep - k

    def panel(a):
        at = sum(nb - k for k in range(4, a))
        return tot[:, sl(at, at + nb - a)]

    own_side(nb, 4, panel, pay_ref, x_scr, r_scr)
    side = side_ref[0]
    y = own_ref[:, sl(1, nb - 2)] - mm(own_ref[:, :B], m[side])
    n3 = lb[pl.ds(pl.multiple_of((2 + side) * B, B), B), :]
    weights = n3 + mm(s_scr[side], x3)
    out_ref[...] = y[:, B:] - mm(y[:, :B], weights)


def own_side(nb, level, m, pay_ref, x_scr, r_scr):
    row = m(level)
    wide = nb - 1 - level
    (s,) = unit_inverse([row[:, :B]], x_scr, r_scr)
    n = mm(s, row[:, B:])
    pay_ref[:, sl(0, 1)] = s
    pay_ref[:, sl(1, 1 + wide)] = n
    at = 1 + wide
    for a in range(level + 1, nb - 1):
        k = a - level
        pay_ref[:, sl(at, at + nb - a)] = m(a) - tn(
            row[:, sl(k, k + 1)], n[:, sl(k - 1, wide)]
        )
        at += nb - a


def merge_kernel(nb, level, split, core_ref, own_ref, *refs):
    refs = list(refs)
    if split:
        kept, fetched = refs[:2]
        full, core = refs[-1], core_ref[0]
        full[core] = kept[...]
        full[1 - core] = fetched[...]
        other = functools.partial(two_part, full, full.shape[2] // B)
        refs = refs[3:-1]
    else:
        whole = refs[0]
        other = lambda i, j: whole[:, sl(i, j)]
        refs = refs[2:]
    after = refs[2:-2]
    pay_ref, x_ref = refs[:2]
    x_scr, r_scr = refs[-2:]
    wide = nb - 1 - level
    q = own_ref[:, sl(1, 1 + wide)] + other(1, 1 + wide)
    x = mm(pair_inverse(own_ref[:, :B], other(0, 1)), q)
    x_ref[...] = x

    def panel(a):
        k = a - level - 1
        at = 1 + wide + sum(nb - j for j in range(level + 1, a))
        return (
            own_ref[:, sl(at, at + nb - a)]
            + other(at, at + nb - a)
            - tn(q[:, sl(k, k + 1)], x[:, sl(k, wide)])
        )

    own_side(nb, level + 1, panel, pay_ref, x_scr, r_scr)
    if after:
        put_half(core_ref, pay_ref, after[0])


def two_part(full, half, i, j):
    if j <= half:
        return full[0, :, sl(i, j)]
    if i >= half:
        return full[1, :, sl(i - half, j - half)]
    return jnp.concatenate([full[0, :, sl(i, half)], full[1, :, sl(0, j - half)]], axis=1)


def put_half(core_ref, pay_ref, half_ref):
    count, half = pay_ref.shape[1] // B, half_ref.shape[1] // B

    @pl.when(core_ref[0] == 0)
    def _():
        half_ref[...] = pay_ref[:, sl(0, half)]

    @pl.when(core_ref[0] == 1)
    def _():
        half_ref[:, sl(0, count - half)] = pay_ref[:, sl(half, count)]
        if 2 * half > count:
            half_ref[:, sl(count - half, half)] = pay_ref[:, sl(count - 1, count)]


def update_kernel(pay_ref, x_ref, y_ref, out_ref):
    wide = x_ref.shape[1]
    weights = pay_ref[:, B : B + wide] + mm(pay_ref[:, :B], x_ref[...])
    out_ref[...] = y_ref[:, B:] - mm(y_ref[:, :B], weights)


def finish_kernel(order_ref, r_ref, own_ref, other_ref, y_ref, out_ref):
    s = own_ref[:, :B]
    n = own_ref[:, B:]
    x = mm(pair_inverse(s, other_ref[:, :B]), n + other_ref[:, B:])
    y = y_ref[:, B:] - mm(y_ref[:, :B], n + mm(s, x))
    pick = (lax.broadcasted_iota(jnp.int32, (B, B), 0) == order_ref[...]).astype(F32)
    out_ref[...] = exact(pick, tn(r_ref[...], y))


def call(kernel, shapes, args, scratch=(), in_specs=None, grid=(), interpret=False):
    shapes = [
        jax.ShapeDtypeStruct((B, w * B) if isinstance(w, int) else w, F32) for w in shapes
    ]
    vmem = pl.BlockSpec(memory_space=pltpu.VMEM)
    one = len(shapes) == 1
    return pl.pallas_call(
        kernel,
        out_shape=shapes[0] if one else shapes,
        grid=grid,
        in_specs=[vmem] * len(args) if in_specs is None else in_specs,
        out_specs=vmem if one else [vmem] * len(shapes),
        scratch_shapes=list(scratch),
        interpret=interpret,
    )(*args)


def swapped(block, axis, bit):
    count = lax.axis_size(axis)
    return lax.ppermute(block, axis, [(k, k ^ (1 << bit)) for k in range(count)])


def pay_width(levels, level):
    return 1 + (levels - level) + sum(levels + 1 - a for a in range(level + 1, levels))


def ring_call(run, levels, side, gathered, rests, own):
    nb = levels + 1
    head, half = cuts(nb)
    active = 2 * levels - 3
    two = [pltpu.VMEM((2, B, B), F32)] * 2
    smem = pl.BlockSpec(memory_space=pltpu.SMEM)
    vmem = pl.BlockSpec(memory_space=pltpu.VMEM)
    anywhere = pl.BlockSpec(memory_space=pl.ANY)
    return run(
        functools.partial(ring_kernel, nb),
        [pay_width(levels, 4), nb - 4],
        [side, gathered, *rests, own],
        [
            pltpu.VMEM((4 * B, active * B), F32),
            pltpu.VMEM((4 * B, (head - active) * B), F32),
            pltpu.VMEM((5 * B, (nb - 4) * B), F32),
            pltpu.VMEM((5 * B, (nb - 4) * B), F32),
            pltpu.VMEM((2, B, (nb - 3) * B), F32),
            pltpu.VMEM((2, B, (nb - 3) * B), F32),
            pltpu.VMEM((2, B, (nb - 3) * B), F32),
            pltpu.VMEM((B, (nb - 4 + 2 * half) * B), F32),
            *two,
            pltpu.VMEM((2, B, B), F32),
            pltpu.SemaphoreType.DMA((2,)),
        ],
        [smem, anywhere] + [vmem] * 5,
    )


def quad_call(run, levels, place, zs, ys):
    nb = levels + 1
    head, half = cuts(nb)
    two = [pltpu.VMEM((2, B, B), F32)] * 2
    smem = pl.BlockSpec(memory_space=pltpu.SMEM)
    anywhere = pl.BlockSpec(memory_space=pl.ANY)
    return run(
        functools.partial(quad_kernel, nb),
        [(B // 4, head * B), (B // 4, half * B), (B // 4, half * B), nb - 2],
        [place, *zs, *ys],
        [
            pltpu.VMEM((4 * B, nb * B), F32),
            pltpu.VMEM((4 * B, nb * B), F32),
            pltpu.VMEM((B, (head + 2 * half) * B), F32),
            *two,
            pltpu.SemaphoreType.DMA((6,)),
        ],
        [smem] + [anywhere] * 6,
    )


def near(x):
    return pltpu.with_memory_space_constraint(x, pltpu.VMEM)


def merge_call(run, levels, level, core, pay, others, behind, half):
    nb = levels + 1
    split = len(others) == 2
    two = [pltpu.VMEM((2, B, B), F32)] * 2
    smem = pl.BlockSpec(memory_space=pltpu.SMEM)
    vmem = pl.BlockSpec(memory_space=pltpu.VMEM)
    anywhere = pl.BlockSpec(memory_space=pl.ANY)
    return run(
        functools.partial(merge_kernel, nb, level, split),
        [pay_width(levels, level + 1), levels - level] + ([half] if half else []),
        [core, pay, *[near(o) for o in others], behind],
        two + ([pltpu.VMEM((2, *others[0].shape), F32)] if split else []),
        [smem] + [vmem] * (1 + len(others)) + [anywhere],
    )


def body(right_sides, leaf_order, leaf_inverse, basis_blocks, interpret=False):
    run = functools.partial(call, interpret=interpret)
    part = functools.partial
    levels = basis_blocks.shape[0]
    nb = levels + 1
    two = [pltpu.VMEM((2, B, B), F32)] * 2
    vmem = pl.BlockSpec(memory_space=pltpu.VMEM)

    z0 = run(part(leaf_kernel, nb), [nb], [leaf_order, leaf_inverse, basis_blocks, right_sides])
    z1 = swapped(z0, "inner", 0)
    z2 = swapped(z0, "inner", 1)
    z3 = swapped(z2, "inner", 0)
    stack = (2 * B, (nb - 1) * B)
    three = [pltpu.VMEM((3, B, B), F32)] * 2
    y01, side = run(part(near_kernel, nb), [stack, nb], [z0, z1, z2], three)
    ys = [y01, run(part(far_kernel, nb), [stack], [z2, z3, side], two)]
    place = lax.axis_index("inner").astype(jnp.int32)
    core = lax.axis_index("outer").astype(jnp.int32) & 1
    mine, rest, send, own = quad_call(run, levels, jnp.stack([place & 3, core]), [z0, z1, z2, z3], ys)
    gathered = lax.all_gather(mine, "inner", tiled=True)
    rest = rest + swapped(send, "outer", 0)
    rest = rest + swapped(rest, "inner", 2)
    rest = rest + swapped(rest, "inner", 3)
    across = swapped(rest, "inner", 1)
    rests = [rest, swapped(rest, "inner", 0), across, swapped(across, "inner", 0)]
    side = jnp.stack([place >> 3, core, place & 3])
    pay, y = ring_call(run, levels, side, gathered, rests, own)
    core = core.reshape(1)
    half = None
    for level in range(4, levels):
        if half is None:
            others = [swapped(pay, "outer", level - 4)]
        else:
            kept = swapped(half, "outer", level - 4)
            others = [kept, swapped(kept, "outer", 0)]
        if level == levels - 1:
            break
        width = pay_width(levels, level + 1)
        cut = -(-width // 2) if width > 6 else 0
        found = merge_call(run, levels, level, core, pay, others, y, cut)
        wide = levels - level
        head = pl.BlockSpec((B, (1 + wide) * B), lambda i: (0, 0))
        y = run(update_kernel, [wide], [pay, found[1], y], (), [head, vmem, vmem], (1,))
        pay = found[0]
        half = found[2] if cut else None
    return run(finish_kernel, [1], [leaf_order, leaf_inverse, pay, near(others[0]), y])


def solution(mesh):
    in_specs = (
        P(("outer", "inner"), None),
        P(("outer", "inner"), None),
        P(("outer", "inner"), None),
        P(None, ("outer", "inner"), None),
    )
    out_specs = P(("outer", "inner"), None)
    return jax.shard_map(body, mesh=mesh, in_specs=in_specs, out_specs=out_specs, check_vma=False)
```

```python
import functools

import jax
import jax.numpy as jnp
from jax import lax
from jax.experimental import pallas as pl
from jax.experimental.pallas import tpu as pltpu
from jax.sharding import PartitionSpec as P

B = 128
F32 = jnp.float32


HIGH = lax.Precision.HIGHEST
HALF = jnp.bfloat16


def product(a, b, axis):
    a_top, b_top = a.astype(HALF), b.astype(HALF)
    a_low = (a - a_top.astype(F32)).astype(HALF)
    b_low = (b - b_top.astype(F32)).astype(HALF)
    left = jnp.concatenate([a_top, a_low, a_top], axis=axis)
    right = jnp.concatenate([b_top, b_top, b_low], axis=0)
    return lax.dot_general(left, right, (((axis,), (0,)), ((), ())), preferred_element_type=F32)


def mm(a, b):
    return product(a, b, 1)


def tn(a, b):
    return product(a, b, 0)


def exact(a, b):
    return jnp.dot(a, b, precision=HIGH, preferred_element_type=F32)


def exact_tn(a, b):
    return lax.dot_general(
        a, b, (((0,), (0,)), ((), ())), precision=HIGH, preferred_element_type=F32
    )


def eye():
    return (
        lax.broadcasted_iota(jnp.int32, (B, B), 0) == lax.broadcasted_iota(jnp.int32, (B, B), 1)
    ).astype(F32)


def sl(i, j):
    return slice(i * B, j * B)


def unit_inverse(grams, x_ref, r_ref):
    unit = eye()
    count = len(grams)
    h = jnp.ones((1, 1), F32)
    for g in grams:
        h = jnp.maximum(
            h, jnp.max(jnp.sum(jnp.abs(g), axis=0, keepdims=True), axis=1, keepdims=True)
        )
    s = 2.0 / h
    s = 2.0 * s * (s + 2.0)
    left = jnp.zeros((1, 1), jnp.int32)
    ahead = s
    for _ in range(14):
        left = left + (ahead < 4000.0).astype(jnp.int32)
        ahead = 2.0 * ahead * (ahead + 2.0)
    steps = jnp.max(left)
    inv_t = 1.0 / (1.0 + s)
    c = 1.0 + inv_t
    scale = 2.0 / (h + 2.0)
    for k, g in enumerate(grams):
        r = (h * unit - 2.0 * g) / (h + 2.0)
        x_ref[k] = (c * scale) * (unit + r)
        r_ref[k] = c * mm(r, r) - inv_t * unit

    def double(_, s):
        s = 2.0 * s * (s + 2.0)
        inv_t = 1.0 / (1.0 + s)
        c = 1.0 + inv_t
        for k in range(count):
            r = r_ref[k]
            x = x_ref[k]
            x_ref[k] = c * (x + mm(x, r))
            r_ref[k] = c * mm(r, r) - inv_t * unit
        return s

    lax.fori_loop(0, steps, double, s)
    found = []
    for k, g in enumerate(grams):
        x = x_ref[k]
        found.append(x + mm(x, unit - x - exact(g, x)))
    return found


def pair_inverse(s_first, s_second):
    unit = eye()
    r = 0.5 * (s_first + s_second - unit)
    t = 7.0
    x = (0.5 * (1.0 + 1.0 / t)) * (unit + r)
    r = (1.0 + 1.0 / t) * mm(r, r) - (1.0 / t) * unit
    for last in (False, False, True):
        t = 2.0 * t * t - 1.0
        c = 1.0 + 1.0 / t
        x = c * (x + mm(x, r))
        if not last:
            r = c * mm(r, r) - (1.0 / t) * unit
    return x


def leaf_kernel(nb, order_ref, r_ref, u_ref, rhs_ref, z_ref):
    pick = (lax.broadcasted_iota(jnp.int32, (B, B), 0) == order_ref[...]).astype(F32)
    r = r_ref[...]
    for b in range(nb - 1):
        z_ref[:, sl(b, b + 1)] = mm(r, u_ref[b])
    z_ref[:, sl(nb - 1, nb)] = mm(r, exact_tn(pick, rhs_ref[...]))


def pair_level(nb, refs, s, n, y_ref):
    x = mm(pair_inverse(s[0], s[1]), n[0] + n[1])
    for i, z in enumerate(refs):
        weights = n[i] + mm(s[i], x)
        y_ref[sl(i, i + 1), :] = z[:, sl(1, nb)] - mm(z[:, sl(0, 1)], weights)


def near_kernel(nb, z0, z1, z2, y_ref, side_ref, x_scr, r_scr):
    refs = (z0, z1, z2)
    p = [tn(z[:, :B], z[...]) for z in refs]
    s = unit_inverse([a[:, :B] for a in p], x_scr, r_scr)
    n = [exact(s[i], p[i][:, B:]) for i in range(3)]
    side_ref[:, :B] = s[2]
    side_ref[:, B:] = n[2]
    pair_level(nb, refs[:2], s, n, y_ref)


def far_kernel(nb, z2, z3, side_ref, y_ref, x_scr, r_scr):
    p = tn(z3[:, :B], z3[...])
    (s,) = unit_inverse([p[:, :B]], x_scr, r_scr)
    n = exact(s, p[:, B:])
    pair_level(nb, (z2, z3), (side_ref[:, :B], s), (side_ref[:, B:], n), y_ref)


def quad_kernel(
    nb, place_ref, zs0, zs1, zs2, zs3, y01, y23,
    out_ref, send_ref, own_ref, z, y, act_ref, x_scr, r_scr, sem,
):
    copies = [
        pltpu.make_async_copy(y01, y.at[pl.ds(0, 2 * B), pl.ds(B, (nb - 1) * B)], sem.at[4]),
        pltpu.make_async_copy(y23, y.at[pl.ds(2 * B, 2 * B), pl.ds(B, (nb - 1) * B)], sem.at[5]),
    ] + [
        pltpu.make_async_copy(
            src.at[:, pl.ds(B, (nb - 1) * B)],
            z.at[pl.ds(i * B, B), pl.ds(B, (nb - 1) * B)],
            sem.at[i],
        )
        for i, src in enumerate((zs0, zs1, zs2, zs3))
    ]
    for copy in copies:
        copy.start()
    for copy in copies:
        copy.wait()
    rows = [slice(0, 2 * B), slice(2 * B, 4 * B)]
    m = [tn(z[rows[n], sl(1, 2)], y[rows[n], sl(1, nb)]) for n in range(2)]
    s = unit_inverse([m[n][:, :B] for n in range(2)], x_scr, r_scr)
    nn = [mm(s[n], m[n][:, B:]) for n in range(2)]
    x = mm(pair_inverse(s[0], s[1]), nn[0] + nn[1])
    last = nb - 1
    for n in range(2):
        weights = nn[n] + mm(s[n], x)
        y[rows[n], sl(2, nb)] = y[rows[n], sl(2, nb)] - mm(y[rows[n], sl(1, 2)], weights)
    m2 = tn(z[:, sl(2, 3)], y[:, sl(2, nb)])
    (s2,) = unit_inverse([m2[:, :B]], x_scr, r_scr)
    n2 = mm(s2, m2[:, B:])
    m3 = tn(z[:, sl(3, 4)], y[:, sl(3, nb)]) - tn(m2[:, sl(1, 2)], n2)
    wide = nb - 3
    act_ref[:, sl(0, 1)] = s2
    act_ref[:, sl(1, 1 + wide)] = n2
    act_ref[:, sl(1 + wide, 1 + 2 * wide)] = m3
    y2 = y[0:B, sl(2, 3)]
    own_ref[:, sl(1, nb - 2)] = y[0:B, sl(3, nb)] - mm(y2, n2)
    own_ref[:, sl(0, 1)] = mm(y2, s2)

    at = 1 + 2 * wide
    for a in range(4, last):
        act_ref[:, sl(at, at + nb - a)] = tn(z[:, sl(a, a + 1)], y[:, sl(a, nb)]) - tn(
            m2[:, sl(a - 2, a - 1)], n2[:, sl(a - 3, wide)]
        )
        at += nb - a
    head, half = cuts(nb)
    first = sl(head, head + half)
    second = sl(head + half, head + 2 * half)
    for part in range(2):
        rows = pl.ds(pl.multiple_of(part * (B // 2) + place_ref[0] * SHARE, SHARE), SHARE)
        put = slice(part * SHARE, (part + 1) * SHARE)
        out_ref[put, sl(0, head)] = act_ref[rows, sl(0, head)]

        @pl.when(place_ref[1] == 0)
        def _():
            out_ref[put, first] = act_ref[rows, first]
            send_ref[put, :] = act_ref[rows, second]

        @pl.when(place_ref[1] == 1)
        def _():
            out_ref[put, first] = act_ref[rows, second]
            send_ref[put, :] = act_ref[rows, first]


SHARE = B // 8


def halve_kernel(cut, bit_ref, out_ref, got_ref, keep_ref, give_ref):
    bit = bit_ref[0]
    for to, at in ((keep_ref, bit), (give_ref, 1 - bit)):
        rows = pl.ds(pl.multiple_of(at * SHARE, SHARE), SHARE)
        to[:, :cut] = out_ref[rows, :cut]
        to[:, cut:] = out_ref[rows, cut:] + got_ref[rows, :]


def cuts(nb):
    rest = sum(nb - a for a in range(5, nb - 1))
    return 1 + 2 * (nb - 3) + nb - 4, rest // 2


def ring_kernel(nb, side_ref, *refs):
    parts, refs = refs[:16], refs[16:]
    own_ref, pay_ref, out_ref, act_ref, pas_ref, la, lb, m, nn, tot, x_scr, r_scr, s_scr = refs
    wide = nb - 3
    deep = nb - 4
    active = 1 + 2 * wide
    for away, share in enumerate(parts):
        at = (side_ref[2] + away) & 15
        rows = pl.ds(pl.multiple_of(at * SHARE, SHARE), SHARE)
        act_ref[rows, :] = share[:, : active * B]
        pas_ref[rows, :] = share[:, active * B :]

    for node in range(2):
        rows = sl(node, node + 1)
        q = act_ref[rows, sl(1, 1 + wide)]
        x = mm(pair_inverse(act_ref[rows, :B], 0.0), q)
        m[node] = x
        lb[rows, :] = x[:, B:]
        la[rows, :] = q[:, B:]
        nn[node] = act_ref[rows, sl(1 + wide, active)] - tn(q[:, :B], x)
    s = unit_inverse([nn[0, :, :B], nn[1, :, :B]], x_scr, r_scr)
    for node in range(2):
        s_scr[node] = s[node]
        la[sl(2 + node, 3 + node), :] = nn[node, :, B:]
        lb[sl(2 + node, 3 + node), :] = mm(s[node], nn[node, :, B:])
    q3 = lb[sl(2, 3), :] + lb[sl(3, 4), :]
    x3 = mm(pair_inverse(s[0], s[1]), q3)
    la[sl(4, 5), :] = q3
    lb[sl(4, 5), :] = x3
    half = cuts(nb)[1]
    tot[...] = jnp.zeros_like(tot)

    def over(part):
        return pas_ref[sl(0, 1), part] + pas_ref[sl(1, 2), part]

    tot[:, sl(0, deep)] = over(sl(0, deep))
    lanes = pl.ds(pl.multiple_of((deep + half * side_ref[1]) * B, B), half * B)
    tot[:, lanes] = over(sl(deep, deep + half))
    at = 0
    for k in range(deep - 1):
        part = sl(at, at + deep - k)
        tot[:, part] = tot[:, part] - tn(la[:, sl(k, k + 1)], lb[:, sl(k, deep)])
        at += deep - k

    def panel(a):
        at = sum(nb - k for k in range(4, a))
        return tot[:, sl(at, at + nb - a)]

    own_side(nb, 4, panel, pay_ref, x_scr, r_scr)
    side = side_ref[0]
    y = own_ref[:, sl(1, nb - 2)] - mm(own_ref[:, :B], m[side])
    n3 = lb[pl.ds(pl.multiple_of((2 + side) * B, B), B), :]
    weights = n3 + mm(s_scr[side], x3)
    out_ref[...] = y[:, B:] - mm(y[:, :B], weights)


def own_side(nb, level, m, pay_ref, x_scr, r_scr):
    row = m(level)
    wide = nb - 1 - level
    (s,) = unit_inverse([row[:, :B]], x_scr, r_scr)
    n = mm(s, row[:, B:])
    pay_ref[:, sl(0, 1)] = s
    pay_ref[:, sl(1, 1 + wide)] = n
    at = 1 + wide
    for a in range(level + 1, nb - 1):
        k = a - level
        pay_ref[:, sl(at, at + nb - a)] = m(a) - tn(
            row[:, sl(k, k + 1)], n[:, sl(k - 1, wide)]
        )
        at += nb - a


def merge_kernel(nb, level, split, core_ref, own_ref, *refs):
    refs = list(refs)
    if split:
        kept, fetched = refs[:2]
        full, core = refs[-1], core_ref[0]
        full[core] = kept[...]
        full[1 - core] = fetched[...]
        other = functools.partial(two_part, full, full.shape[2] // B)
        refs = refs[3:-1]
    else:
        whole = refs[0]
        other = lambda i, j: whole[:, sl(i, j)]
        refs = refs[2:]
    after = refs[2:-2]
    pay_ref, x_ref = refs[:2]
    x_scr, r_scr = refs[-2:]
    wide = nb - 1 - level
    q = own_ref[:, sl(1, 1 + wide)] + other(1, 1 + wide)
    x = mm(pair_inverse(own_ref[:, :B], other(0, 1)), q)
    x_ref[...] = x

    def panel(a):
        k = a - level - 1
        at = 1 + wide + sum(nb - j for j in range(level + 1, a))
        return (
            own_ref[:, sl(at, at + nb - a)]
            + other(at, at + nb - a)
            - tn(q[:, sl(k, k + 1)], x[:, sl(k, wide)])
        )

    own_side(nb, level + 1, panel, pay_ref, x_scr, r_scr)
    if after:
        put_half(core_ref, pay_ref, after[0])


def two_part(full, half, i, j):
    if j <= half:
        return full[0, :, sl(i, j)]
    if i >= half:
        return full[1, :, sl(i - half, j - half)]
    return jnp.concatenate([full[0, :, sl(i, half)], full[1, :, sl(0, j - half)]], axis=1)


def put_half(core_ref, pay_ref, half_ref):
    count, half = pay_ref.shape[1] // B, half_ref.shape[1] // B

    @pl.when(core_ref[0] == 0)
    def _():
        half_ref[...] = pay_ref[:, sl(0, half)]

    @pl.when(core_ref[0] == 1)
    def _():
        half_ref[:, sl(0, count - half)] = pay_ref[:, sl(half, count)]
        if 2 * half > count:
            half_ref[:, sl(count - half, half)] = pay_ref[:, sl(count - 1, count)]


def update_kernel(pay_ref, x_ref, y_ref, out_ref):
    wide = x_ref.shape[1]
    weights = pay_ref[:, B : B + wide] + mm(pay_ref[:, :B], x_ref[...])
    out_ref[...] = y_ref[:, B:] - mm(y_ref[:, :B], weights)


def finish_kernel(order_ref, r_ref, own_ref, other_ref, y_ref, out_ref):
    s = own_ref[:, :B]
    n = own_ref[:, B:]
    x = mm(pair_inverse(s, other_ref[:, :B]), n + other_ref[:, B:])
    y = y_ref[:, B:] - mm(y_ref[:, :B], n + mm(s, x))
    pick = (lax.broadcasted_iota(jnp.int32, (B, B), 0) == order_ref[...]).astype(F32)
    out_ref[...] = exact(pick, tn(r_ref[...], y))


def call(kernel, shapes, args, scratch=(), in_specs=None, grid=(), interpret=False):
    shapes = [
        jax.ShapeDtypeStruct((B, w * B) if isinstance(w, int) else w, F32) for w in shapes
    ]
    vmem = pl.BlockSpec(memory_space=pltpu.VMEM)
    one = len(shapes) == 1
    return pl.pallas_call(
        kernel,
        out_shape=shapes[0] if one else shapes,
        grid=grid,
        in_specs=[vmem] * len(args) if in_specs is None else in_specs,
        out_specs=vmem if one else [vmem] * len(shapes),
        scratch_shapes=list(scratch),
        interpret=interpret,
    )(*args)


def swapped(block, axis, bit):
    count = lax.axis_size(axis)
    return lax.ppermute(block, axis, [(k, k ^ (1 << bit)) for k in range(count)])


def pay_width(levels, level):
    return 1 + (levels - level) + sum(levels + 1 - a for a in range(level + 1, levels))


def ring_call(run, levels, side, parts, own):
    nb = levels + 1
    head, half = cuts(nb)
    active = 2 * levels - 3
    two = [pltpu.VMEM((2, B, B), F32)] * 2
    smem = pl.BlockSpec(memory_space=pltpu.SMEM)
    vmem = pl.BlockSpec(memory_space=pltpu.VMEM)
    return run(
        functools.partial(ring_kernel, nb),
        [pay_width(levels, 4), nb - 4],
        [side, *parts, own],
        [
            pltpu.VMEM((2 * B, active * B), F32),
            pltpu.VMEM((2 * B, (head + half - active) * B), F32),
            pltpu.VMEM((5 * B, (nb - 4) * B), F32),
            pltpu.VMEM((5 * B, (nb - 4) * B), F32),
            pltpu.VMEM((2, B, (nb - 3) * B), F32),
            pltpu.VMEM((2, B, (nb - 3) * B), F32),
            pltpu.VMEM((B, (nb - 4 + 2 * half) * B), F32),
            *two,
            pltpu.VMEM((2, B, B), F32),
        ],
        [smem] + [vmem] * 17,
    )


def quad_call(run, levels, place, zs, ys):
    nb = levels + 1
    head, half = cuts(nb)
    two = [pltpu.VMEM((2, B, B), F32)] * 2
    smem = pl.BlockSpec(memory_space=pltpu.SMEM)
    anywhere = pl.BlockSpec(memory_space=pl.ANY)
    return run(
        functools.partial(quad_kernel, nb),
        [(2 * SHARE, (head + half) * B), (2 * SHARE, half * B), nb - 2],
        [place, *zs, *ys],
        [
            pltpu.VMEM((4 * B, nb * B), F32),
            pltpu.VMEM((4 * B, nb * B), F32),
            pltpu.VMEM((B, (head + 2 * half) * B), F32),
            *two,
            pltpu.SemaphoreType.DMA((6,)),
        ],
        [smem] + [anywhere] * 6,
    )


def near(x):
    return pltpu.with_memory_space_constraint(x, pltpu.VMEM)


def merge_call(run, levels, level, core, pay, others, behind, half):
    nb = levels + 1
    split = len(others) == 2
    two = [pltpu.VMEM((2, B, B), F32)] * 2
    smem = pl.BlockSpec(memory_space=pltpu.SMEM)
    vmem = pl.BlockSpec(memory_space=pltpu.VMEM)
    anywhere = pl.BlockSpec(memory_space=pl.ANY)
    return run(
        functools.partial(merge_kernel, nb, level, split),
        [pay_width(levels, level + 1), levels - level] + ([half] if half else []),
        [core, pay, *[near(o) for o in others], behind],
        two + ([pltpu.VMEM((2, *others[0].shape), F32)] if split else []),
        [smem] + [vmem] * (1 + len(others)) + [anywhere],
    )


def body(right_sides, leaf_order, leaf_inverse, basis_blocks, interpret=False):
    run = functools.partial(call, interpret=interpret)
    part = functools.partial
    levels = basis_blocks.shape[0]
    nb = levels + 1
    two = [pltpu.VMEM((2, B, B), F32)] * 2
    vmem = pl.BlockSpec(memory_space=pltpu.VMEM)

    z0 = run(part(leaf_kernel, nb), [nb], [leaf_order, leaf_inverse, basis_blocks, right_sides])
    z1 = swapped(z0, "inner", 0)
    z2 = swapped(z0, "inner", 1)
    z3 = swapped(z2, "inner", 0)
    stack = (2 * B, (nb - 1) * B)
    three = [pltpu.VMEM((3, B, B), F32)] * 2
    y01, side = run(part(near_kernel, nb), [stack, nb], [z0, z1, z2], three)
    ys = [y01, run(part(far_kernel, nb), [stack], [z2, z3, side], two)]
    place = lax.axis_index("inner").astype(jnp.int32)
    core = lax.axis_index("outer").astype(jnp.int32) & 1
    mine, send, own = quad_call(run, levels, jnp.stack([place & 3, core]), [z0, z1, z2, z3], ys)
    half = (SHARE, mine.shape[1])
    keep, give = run(
        part(halve_kernel, cuts(nb)[0] * B),
        [half, half],
        [(place >> 2 & 1).reshape(1), mine, near(swapped(send, "outer", 0))],
        (),
        [pl.BlockSpec(memory_space=pltpu.SMEM)] + [pl.BlockSpec(memory_space=pltpu.VMEM)] * 2,
    )
    mine = keep + swapped(give, "inner", 2)
    parts = [mine] + [None] * 15
    up = down = mine
    for step in range(1, 9):
        up = lax.ppermute(up, "inner", [(k, (k + 1) % 16) for k in range(16)])
        parts[16 - step] = up
        if step < 8:
            down = lax.ppermute(down, "inner", [(k, (k - 1) % 16) for k in range(16)])
            parts[step] = down
    side = jnp.stack([place >> 3, core, place])
    pay, y = ring_call(run, levels, side, parts, own)
    core = core.reshape(1)
    half = None
    for level in range(4, levels):
        if half is None:
            others = [swapped(pay, "outer", level - 4)]
        else:
            kept = swapped(half, "outer", level - 4)
            others = [kept, swapped(kept, "outer", 0)]
        if level == levels - 1:
            break
        width = pay_width(levels, level + 1)
        cut = -(-width // 2) if width > 6 else 0
        found = merge_call(run, levels, level, core, pay, others, y, cut)
        wide = levels - level
        head = pl.BlockSpec((B, (1 + wide) * B), lambda i: (0, 0))
        y = run(update_kernel, [wide], [pay, found[1], y], (), [head, vmem, vmem], (1,))
        pay = found[0]
        half = found[2] if cut else None
    return run(finish_kernel, [1], [leaf_order, leaf_inverse, pay, near(others[0]), y])


def solution(mesh):
    in_specs = (
        P(("outer", "inner"), None),
        P(("outer", "inner"), None),
        P(("outer", "inner"), None),
        P(None, ("outer", "inner"), None),
    )
    out_specs = P(("outer", "inner"), None)
    return jax.shard_map(body, mesh=mesh, in_specs=in_specs, out_specs=out_specs, check_vma=False)
```

```python
import functools

import jax
import jax.numpy as jnp
from jax import lax
from jax.experimental import pallas as pl
from jax.experimental.pallas import tpu as pltpu
from jax.sharding import PartitionSpec as P

B = 128
F32 = jnp.float32


HIGH = lax.Precision.HIGHEST
HALF = jnp.bfloat16


def product(a, b, axis):
    a_top, b_top = a.astype(HALF), b.astype(HALF)
    a_low = (a - a_top.astype(F32)).astype(HALF)
    b_low = (b - b_top.astype(F32)).astype(HALF)
    left = jnp.concatenate([a_top, a_low, a_top], axis=axis)
    right = jnp.concatenate([b_top, b_top, b_low], axis=0)
    return lax.dot_general(left, right, (((axis,), (0,)), ((), ())), preferred_element_type=F32)


def mm(a, b):
    return product(a, b, 1)


def tn(a, b):
    return product(a, b, 0)


def exact(a, b):
    return jnp.dot(a, b, precision=HIGH, preferred_element_type=F32)


def exact_tn(a, b):
    return lax.dot_general(
        a, b, (((0,), (0,)), ((), ())), precision=HIGH, preferred_element_type=F32
    )


def eye():
    return (
        lax.broadcasted_iota(jnp.int32, (B, B), 0) == lax.broadcasted_iota(jnp.int32, (B, B), 1)
    ).astype(F32)


def sl(i, j):
    return slice(i * B, j * B)


def unit_inverse(grams, x_ref, r_ref):
    unit = eye()
    count = len(grams)
    h = jnp.ones((1, 1), F32)
    for g in grams:
        h = jnp.maximum(
            h, jnp.max(jnp.sum(jnp.abs(g), axis=0, keepdims=True), axis=1, keepdims=True)
        )
    s = 2.0 / h
    s = 2.0 * s * (s + 2.0)
    left = jnp.zeros((1, 1), jnp.int32)
    ahead = s
    for _ in range(14):
        left = left + (ahead < 4000.0).astype(jnp.int32)
        ahead = 2.0 * ahead * (ahead + 2.0)
    steps = jnp.max(left)
    inv_t = 1.0 / (1.0 + s)
    c = 1.0 + inv_t
    scale = 2.0 / (h + 2.0)
    for k, g in enumerate(grams):
        r = (h * unit - 2.0 * g) / (h + 2.0)
        x_ref[k] = (c * scale) * (unit + r)
        r_ref[k] = c * mm(r, r) - inv_t * unit

    def double(_, s):
        s = 2.0 * s * (s + 2.0)
        inv_t = 1.0 / (1.0 + s)
        c = 1.0 + inv_t
        for k in range(count):
            r = r_ref[k]
            x = x_ref[k]
            x_ref[k] = c * (x + mm(x, r))
            r_ref[k] = c * mm(r, r) - inv_t * unit
        return s

    lax.fori_loop(0, steps, double, s)
    found = []
    for k, g in enumerate(grams):
        x = x_ref[k]
        found.append(x + mm(x, unit - x - exact(g, x)))
    return found


def pair_inverse(s_first, s_second):
    unit = eye()
    r = 0.5 * (s_first + s_second - unit)
    t = 7.0
    x = (0.5 * (1.0 + 1.0 / t)) * (unit + r)
    r = (1.0 + 1.0 / t) * mm(r, r) - (1.0 / t) * unit
    for last in (False, False, True):
        t = 2.0 * t * t - 1.0
        c = 1.0 + 1.0 / t
        x = c * (x + mm(x, r))
        if not last:
            r = c * mm(r, r) - (1.0 / t) * unit
    return x


def leaf_kernel(nb, order_ref, r_ref, u_ref, rhs_ref, z_ref):
    pick = (lax.broadcasted_iota(jnp.int32, (B, B), 0) == order_ref[...]).astype(F32)
    r = r_ref[...]
    for b in range(nb - 1):
        z_ref[:, sl(b, b + 1)] = mm(r, u_ref[b])
    z_ref[:, sl(nb - 1, nb)] = mm(r, exact_tn(pick, rhs_ref[...]))


def pair_level(nb, refs, s, n, y_ref):
    x = mm(pair_inverse(s[0], s[1]), n[0] + n[1])
    for i, z in enumerate(refs):
        weights = n[i] + mm(s[i], x)
        y_ref[sl(i, i + 1), :] = z[:, sl(1, nb)] - mm(z[:, sl(0, 1)], weights)


def near_kernel(nb, z0, z1, z2, y_ref, side_ref, x_scr, r_scr):
    refs = (z0, z1, z2)
    p = [tn(z[:, :B], z[...]) for z in refs]
    s = unit_inverse([a[:, :B] for a in p], x_scr, r_scr)
    n = [exact(s[i], p[i][:, B:]) for i in range(3)]
    side_ref[:, :B] = s[2]
    side_ref[:, B:] = n[2]
    pair_level(nb, refs[:2], s, n, y_ref)


def far_kernel(nb, z2, z3, side_ref, y_ref, x_scr, r_scr):
    p = tn(z3[:, :B], z3[...])
    (s,) = unit_inverse([p[:, :B]], x_scr, r_scr)
    n = exact(s, p[:, B:])
    pair_level(nb, (z2, z3), (side_ref[:, :B], s), (side_ref[:, B:], n), y_ref)


def quad_kernel(
    nb, place_ref, zs0, zs1, zs2, zs3, y01, y23,
    hold_ref, give_ref, keep_ref, send_ref, own_ref, z, y, act_ref, x_scr, r_scr, sem,
):
    copies = [
        pltpu.make_async_copy(y01, y.at[pl.ds(0, 2 * B), pl.ds(B, (nb - 1) * B)], sem.at[4]),
        pltpu.make_async_copy(y23, y.at[pl.ds(2 * B, 2 * B), pl.ds(B, (nb - 1) * B)], sem.at[5]),
    ] + [
        pltpu.make_async_copy(
            src.at[:, pl.ds(B, (nb - 1) * B)],
            z.at[pl.ds(i * B, B), pl.ds(B, (nb - 1) * B)],
            sem.at[i],
        )
        for i, src in enumerate((zs0, zs1, zs2, zs3))
    ]
    for copy in copies:
        copy.start()
    for copy in copies:
        copy.wait()
    rows = [slice(0, 2 * B), slice(2 * B, 4 * B)]
    m = [tn(z[rows[n], sl(1, 2)], y[rows[n], sl(1, nb)]) for n in range(2)]
    s = unit_inverse([m[n][:, :B] for n in range(2)], x_scr, r_scr)
    nn = [mm(s[n], m[n][:, B:]) for n in range(2)]
    x = mm(pair_inverse(s[0], s[1]), nn[0] + nn[1])
    last = nb - 1
    for n in range(2):
        weights = nn[n] + mm(s[n], x)
        y[rows[n], sl(2, nb)] = y[rows[n], sl(2, nb)] - mm(y[rows[n], sl(1, 2)], weights)
    m2 = tn(z[:, sl(2, 3)], y[:, sl(2, nb)])
    (s2,) = unit_inverse([m2[:, :B]], x_scr, r_scr)
    n2 = mm(s2, m2[:, B:])
    m3 = tn(z[:, sl(3, 4)], y[:, sl(3, nb)]) - tn(m2[:, sl(1, 2)], n2)
    wide = nb - 3
    act_ref[:, sl(0, 1)] = s2
    act_ref[:, sl(1, 1 + wide)] = n2
    act_ref[:, sl(1 + wide, 1 + 2 * wide)] = m3
    y2 = y[0:B, sl(2, 3)]
    own_ref[:, sl(1, nb - 2)] = y[0:B, sl(3, nb)] - mm(y2, n2)
    own_ref[:, sl(0, 1)] = mm(y2, s2)

    at = 1 + 2 * wide
    for a in range(4, last):
        act_ref[:, sl(at, at + nb - a)] = tn(z[:, sl(a, a + 1)], y[:, sl(a, nb)]) - tn(
            m2[:, sl(a - 2, a - 1)], n2[:, sl(a - 3, wide)]
        )
        at += nb - a
    head, half = cuts(nb)
    first = sl(head, head + half)
    second = sl(head + half, head + 2 * half)
    for part in range(2):
        rows = pl.ds(pl.multiple_of(part * (B // 2) + place_ref[0] * SHARE, SHARE), SHARE)
        put = slice(part * SHARE, (part + 1) * SHARE)

        @pl.when(place_ref[2] == part)
        def _():
            hold_ref[...] = act_ref[rows, sl(0, head)]

        @pl.when(place_ref[2] != part)
        def _():
            give_ref[...] = act_ref[rows, sl(0, head)]

        @pl.when(place_ref[1] == 0)
        def _():
            keep_ref[put, :] = act_ref[rows, first]
            send_ref[put, :] = act_ref[rows, second]

        @pl.when(place_ref[1] == 1)
        def _():
            keep_ref[put, :] = act_ref[rows, second]
            send_ref[put, :] = act_ref[rows, first]


SHARE = B // 8


def halve_kernel(bit_ref, mine_ref, got_ref, keep_ref, give_ref):
    bit = bit_ref[0]
    for to, at in ((keep_ref, bit), (give_ref, 1 - bit)):
        rows = pl.ds(pl.multiple_of(at * SHARE, SHARE), SHARE)
        to[...] = mine_ref[rows, :] + got_ref[rows, :]


def cuts(nb):
    rest = sum(nb - a for a in range(5, nb - 1))
    return 1 + 2 * (nb - 3) + nb - 4, rest // 2


def ring_kernel(nb, side_ref, *refs):
    parts, refs = refs[:16], refs[16:]
    own_ref, pay_ref, out_ref, act_ref, pas_ref, la, lb, m, nn, tot, x_scr, r_scr, s_scr = refs
    wide = nb - 3
    deep = nb - 4
    active = 1 + 2 * wide
    for away, share in enumerate(parts):
        at = (side_ref[2] + away) & 15
        rows = pl.ds(pl.multiple_of(at * SHARE, SHARE), SHARE)
        act_ref[rows, :] = share[:, : active * B]
        pas_ref[rows, :] = share[:, active * B :]

    for node in range(2):
        rows = sl(node, node + 1)
        q = act_ref[rows, sl(1, 1 + wide)]
        x = mm(pair_inverse(act_ref[rows, :B], 0.0), q)
        m[node] = x
        lb[rows, :] = x[:, B:]
        la[rows, :] = q[:, B:]
        nn[node] = act_ref[rows, sl(1 + wide, active)] - tn(q[:, :B], x)
    s = unit_inverse([nn[0, :, :B], nn[1, :, :B]], x_scr, r_scr)
    for node in range(2):
        s_scr[node] = s[node]
        la[sl(2 + node, 3 + node), :] = nn[node, :, B:]
        lb[sl(2 + node, 3 + node), :] = mm(s[node], nn[node, :, B:])
    q3 = lb[sl(2, 3), :] + lb[sl(3, 4), :]
    x3 = mm(pair_inverse(s[0], s[1]), q3)
    la[sl(4, 5), :] = q3
    lb[sl(4, 5), :] = x3
    half = cuts(nb)[1]
    tot[...] = jnp.zeros_like(tot)

    def over(part):
        return pas_ref[sl(0, 1), part] + pas_ref[sl(1, 2), part]

    tot[:, sl(0, deep)] = over(sl(0, deep))
    lanes = pl.ds(pl.multiple_of((deep + half * side_ref[1]) * B, B), half * B)
    tot[:, lanes] = over(sl(deep, deep + half))
    at = 0
    for k in range(deep - 1):
        part = sl(at, at + deep - k)
        tot[:, part] = tot[:, part] - tn(la[:, sl(k, k + 1)], lb[:, sl(k, deep)])
        at += deep - k

    def panel(a):
        at = sum(nb - k for k in range(4, a))
        return tot[:, sl(at, at + nb - a)]

    own_side(nb, 4, panel, pay_ref, x_scr, r_scr)
    side = side_ref[0]
    y = own_ref[:, sl(1, nb - 2)] - mm(own_ref[:, :B], m[side])
    n3 = lb[pl.ds(pl.multiple_of((2 + side) * B, B), B), :]
    weights = n3 + mm(s_scr[side], x3)
    out_ref[...] = y[:, B:] - mm(y[:, :B], weights)


def own_side(nb, level, m, pay_ref, x_scr, r_scr):
    row = m(level)
    wide = nb - 1 - level
    (s,) = unit_inverse([row[:, :B]], x_scr, r_scr)
    n = mm(s, row[:, B:])
    pay_ref[:, sl(0, 1)] = s
    pay_ref[:, sl(1, 1 + wide)] = n
    at = 1 + wide
    for a in range(level + 1, nb - 1):
        k = a - level
        pay_ref[:, sl(at, at + nb - a)] = m(a) - tn(
            row[:, sl(k, k + 1)], n[:, sl(k - 1, wide)]
        )
        at += nb - a


def merge_kernel(nb, level, split, core_ref, own_ref, *refs):
    refs = list(refs)
    if split:
        kept, fetched = refs[:2]
        full, core = refs[-1], core_ref[0]
        full[core] = kept[...]
        full[1 - core] = fetched[...]
        other = functools.partial(two_part, full, full.shape[2] // B)
        refs = refs[3:-1]
    else:
        whole = refs[0]
        other = lambda i, j: whole[:, sl(i, j)]
        refs = refs[2:]
    after = refs[2:-2]
    pay_ref, x_ref = refs[:2]
    x_scr, r_scr = refs[-2:]
    wide = nb - 1 - level
    q = own_ref[:, sl(1, 1 + wide)] + other(1, 1 + wide)
    x = mm(pair_inverse(own_ref[:, :B], other(0, 1)), q)
    x_ref[...] = x

    def panel(a):
        k = a - level - 1
        at = 1 + wide + sum(nb - j for j in range(level + 1, a))
        return (
            own_ref[:, sl(at, at + nb - a)]
            + other(at, at + nb - a)
            - tn(q[:, sl(k, k + 1)], x[:, sl(k, wide)])
        )

    own_side(nb, level + 1, panel, pay_ref, x_scr, r_scr)
    if after:
        put_half(core_ref, pay_ref, after[0])


def two_part(full, half, i, j):
    if j <= half:
        return full[0, :, sl(i, j)]
    if i >= half:
        return full[1, :, sl(i - half, j - half)]
    return jnp.concatenate([full[0, :, sl(i, half)], full[1, :, sl(0, j - half)]], axis=1)


def put_half(core_ref, pay_ref, half_ref):
    count, half = pay_ref.shape[1] // B, half_ref.shape[1] // B

    @pl.when(core_ref[0] == 0)
    def _():
        half_ref[...] = pay_ref[:, sl(0, half)]

    @pl.when(core_ref[0] == 1)
    def _():
        half_ref[:, sl(0, count - half)] = pay_ref[:, sl(half, count)]
        if 2 * half > count:
            half_ref[:, sl(count - half, half)] = pay_ref[:, sl(count - 1, count)]


def update_kernel(pay_ref, x_ref, y_ref, out_ref):
    wide = x_ref.shape[1]
    weights = pay_ref[:, B : B + wide] + mm(pay_ref[:, :B], x_ref[...])
    out_ref[...] = y_ref[:, B:] - mm(y_ref[:, :B], weights)


def finish_kernel(order_ref, r_ref, own_ref, other_ref, y_ref, out_ref):
    s = own_ref[:, :B]
    n = own_ref[:, B:]
    x = mm(pair_inverse(s, other_ref[:, :B]), n + other_ref[:, B:])
    y = y_ref[:, B:] - mm(y_ref[:, :B], n + mm(s, x))
    pick = (lax.broadcasted_iota(jnp.int32, (B, B), 0) == order_ref[...]).astype(F32)
    out_ref[...] = exact(pick, tn(r_ref[...], y))


def call(kernel, shapes, args, scratch=(), in_specs=None, grid=(), interpret=False):
    shapes = [
        jax.ShapeDtypeStruct((B, w * B) if isinstance(w, int) else w, F32) for w in shapes
    ]
    vmem = pl.BlockSpec(memory_space=pltpu.VMEM)
    one = len(shapes) == 1
    return pl.pallas_call(
        kernel,
        out_shape=shapes[0] if one else shapes,
        grid=grid,
        in_specs=[vmem] * len(args) if in_specs is None else in_specs,
        out_specs=vmem if one else [vmem] * len(shapes),
        scratch_shapes=list(scratch),
        interpret=interpret,
    )(*args)


def swapped(block, axis, bit):
    count = lax.axis_size(axis)
    return lax.ppermute(block, axis, [(k, k ^ (1 << bit)) for k in range(count)])


def pay_width(levels, level):
    return 1 + (levels - level) + sum(levels + 1 - a for a in range(level + 1, levels))


def ring_call(run, levels, side, parts, own):
    nb = levels + 1
    head, half = cuts(nb)
    active = 2 * levels - 3
    two = [pltpu.VMEM((2, B, B), F32)] * 2
    smem = pl.BlockSpec(memory_space=pltpu.SMEM)
    vmem = pl.BlockSpec(memory_space=pltpu.VMEM)
    return run(
        functools.partial(ring_kernel, nb),
        [pay_width(levels, 4), nb - 4],
        [side, *parts, own],
        [
            pltpu.VMEM((2 * B, active * B), F32),
            pltpu.VMEM((2 * B, (head + half - active) * B), F32),
            pltpu.VMEM((5 * B, (nb - 4) * B), F32),
            pltpu.VMEM((5 * B, (nb - 4) * B), F32),
            pltpu.VMEM((2, B, (nb - 3) * B), F32),
            pltpu.VMEM((2, B, (nb - 3) * B), F32),
            pltpu.VMEM((B, (nb - 4 + 2 * half) * B), F32),
            *two,
            pltpu.VMEM((2, B, B), F32),
        ],
        [smem] + [vmem] * 17,
    )


def quad_call(run, levels, place, zs, ys):
    nb = levels + 1
    head, half = cuts(nb)
    two = [pltpu.VMEM((2, B, B), F32)] * 2
    smem = pl.BlockSpec(memory_space=pltpu.SMEM)
    anywhere = pl.BlockSpec(memory_space=pl.ANY)
    return run(
        functools.partial(quad_kernel, nb),
        [(SHARE, head * B)] * 2 + [(2 * SHARE, half * B)] * 2 + [nb - 2],
        [place, *zs, *ys],
        [
            pltpu.VMEM((4 * B, nb * B), F32),
            pltpu.VMEM((4 * B, nb * B), F32),
            pltpu.VMEM((B, (head + 2 * half) * B), F32),
            *two,
            pltpu.SemaphoreType.DMA((6,)),
        ],
        [smem] + [anywhere] * 6,
    )


def near(x):
    return pltpu.with_memory_space_constraint(x, pltpu.VMEM)


def merge_call(run, levels, level, core, pay, others, behind, half):
    nb = levels + 1
    split = len(others) == 2
    two = [pltpu.VMEM((2, B, B), F32)] * 2
    smem = pl.BlockSpec(memory_space=pltpu.SMEM)
    vmem = pl.BlockSpec(memory_space=pltpu.VMEM)
    anywhere = pl.BlockSpec(memory_space=pl.ANY)
    return run(
        functools.partial(merge_kernel, nb, level, split),
        [pay_width(levels, level + 1), levels - level] + ([half] if half else []),
        [core, pay, *[near(o) for o in others], behind],
        two + ([pltpu.VMEM((2, *others[0].shape), F32)] if split else []),
        [smem] + [vmem] * (1 + len(others)) + [anywhere],
    )


def body(right_sides, leaf_order, leaf_inverse, basis_blocks, interpret=False):
    run = functools.partial(call, interpret=interpret)
    part = functools.partial
    levels = basis_blocks.shape[0]
    nb = levels + 1
    two = [pltpu.VMEM((2, B, B), F32)] * 2
    vmem = pl.BlockSpec(memory_space=pltpu.VMEM)

    z0 = run(part(leaf_kernel, nb), [nb], [leaf_order, leaf_inverse, basis_blocks, right_sides])
    z1 = swapped(z0, "inner", 0)
    z2 = swapped(z0, "inner", 1)
    z3 = swapped(z2, "inner", 0)
    stack = (2 * B, (nb - 1) * B)
    three = [pltpu.VMEM((3, B, B), F32)] * 2
    y01, side = run(part(near_kernel, nb), [stack, nb], [z0, z1, z2], three)
    ys = [y01, run(part(far_kernel, nb), [stack], [z2, z3, side], two)]
    place = lax.axis_index("inner").astype(jnp.int32)
    core = lax.axis_index("outer").astype(jnp.int32) & 1
    bit = place >> 2 & 1
    hold, give, rest, send, own = quad_call(
        run, levels, jnp.stack([place & 3, core, bit]), [z0, z1, z2, z3], ys
    )
    hold = hold + swapped(give, "inner", 2)
    half = (SHARE, rest.shape[1])
    keep, give = run(
        halve_kernel,
        [half, half],
        [bit.reshape(1), rest, near(swapped(send, "outer", 0))],
        (),
        [pl.BlockSpec(memory_space=pltpu.SMEM)] + [pl.BlockSpec(memory_space=pltpu.VMEM)] * 2,
    )
    mine = jnp.concatenate([hold, keep + swapped(give, "inner", 2)], axis=1)
    parts = [mine] + [None] * 15
    up = down = mine
    for step in range(1, 9):
        up = lax.ppermute(up, "inner", [(k, (k + 1) % 16) for k in range(16)])
        parts[16 - step] = up
        if step < 8:
            down = lax.ppermute(down, "inner", [(k, (k - 1) % 16) for k in range(16)])
            parts[step] = down
    side = jnp.stack([place >> 3, core, place])
    pay, y = ring_call(run, levels, side, parts, own)
    core = core.reshape(1)
    half = None
    for level in range(4, levels):
        if half is None:
            others = [swapped(pay, "outer", level - 4)]
        else:
            kept = swapped(half, "outer", level - 4)
            others = [kept, swapped(kept, "outer", 0)]
        if level == levels - 1:
            break
        width = pay_width(levels, level + 1)
        cut = -(-width // 2) if width > 6 else 0
        found = merge_call(run, levels, level, core, pay, others, y, cut)
        wide = levels - level
        head = pl.BlockSpec((B, (1 + wide) * B), lambda i: (0, 0))
        y = run(update_kernel, [wide], [pay, found[1], y], (), [head, vmem, vmem], (1,))
        pay = found[0]
        half = found[2] if cut else None
    return run(finish_kernel, [1], [leaf_order, leaf_inverse, pay, near(others[0]), y])


def solution(mesh):
    in_specs = (
        P(("outer", "inner"), None),
        P(("outer", "inner"), None),
        P(("outer", "inner"), None),
        P(None, ("outer", "inner"), None),
    )
    out_specs = P(("outer", "inner"), None)
    return jax.shard_map(body, mesh=mesh, in_specs=in_specs, out_specs=out_specs, check_vma=False)
```
